256 devices in a mesh: slab: 4 (over x), energy: 64 (over y, z, core).
Axes of the slice: x: 4, y: 4, z: 8, core: 2. Of those that a mesh axis runs over, the one named last changes fastest.
Arguments:
- energies: float32 [64], P('energy'), may hold values from -1 to 1
- broadening: float32 [64], P('energy'), may hold values from 0.3 to 1
- hamiltonian: float32 [1024, 256], P('slab'), as said below
- coupling: float32 [1024, 256], P('slab'), may hold values from -0.21875 to 0.21875
- propagator: float32 [2, 6, 64, 64], replicated, may hold values from -0.75 to 0.75
- neighbors: int32 [1024, 32], P('slab'), may hold values from 0 to 255, as said below
- phonon_modes: int32 [1024, 32], P('slab'), may hold values from 0 to 5
Outputs:
- green_blocks: float32 [64, 2, 1024, 256], P('energy', None, 'slab')
- self_energy: float32 [64, 2, 32768], P('energy', None, 'slab')
The draws below stay inside these ranges and needn't reach their ends.
Inputs may be any that keep to these rules, and one draw needn't show every extreme that they name: `hamiltonian`: each block of 256 rows is symmetric. `neighbors`: an orbital is never its own neighbour.
All inputs are finite; a program needn't handle non-finite values.
Results may differ from the reference program's by a relative error of at most 0.0001.
Values sent between devices are 32-bit elements; how exact they have to be, the bound alone decides.
No kernel may reach another device: no remote copies, remote signals or barrier semaphores. Data moves between devices by JAX's collectives and lax.ppermute only.
A program may use at most 128 MiB of HBM per device.

```python
import math
import jax
import jax.numpy as jnp
from jax import lax

B = 256
NEIGH = 32
MODES = 6
ENERGIES = 64
ORB = 1024


def draw_hamiltonian(key, part):
    key_site = jax.random.fold_in(key, 11)
    key_hop = jax.random.fold_in(key, 12)
    block_count = ORB // B
    spread = 0.3 / math.sqrt(B)
    hopping = jax.random.normal(key_hop, (block_count, B, B), jnp.float32) * spread
    hopping = jnp.clip(hopping, -6.0 * spread, 6.0 * spread)
    identity = jnp.eye(B, dtype=jnp.float32)
    symmetric = (hopping + jnp.swapaxes(hopping, 1, 2)) / math.sqrt(2.0) * (1.0 - identity)
    onsite = jax.random.uniform(key_site, (block_count, B), jnp.float32, -3.0, -2.0)
    return (symmetric + identity * onsite[:, :, None]).reshape(ORB, B)


def draw_neighbors(key, part):
    offsets = jax.random.randint(jax.random.fold_in(key, 21), (ORB, NEIGH), 1, B)
    positions = (jnp.arange(ORB, dtype=jnp.int32) % B)[:, None]
    return ((positions + offsets) % B).astype(jnp.int32)


def set_ends(array, rng, least, high):
    longest = array.shape.index(max(array.shape))
    spots = []
    for shift in (0, 1):
        where = [jax.random.randint(jax.random.fold_in(rng, axis), (), 0, length) for axis, length in enumerate(array.shape)]
        where[longest] = (where[longest] + shift) % array.shape[longest]
        spots.append(tuple(where))
    return array.at[spots[0]].set(least).at[spots[1]].set(high)


def shard_levels(rng, shape, cuts, least, top_value):
    loudness, own = 1.0, jax.random.fold_in(rng, 6)
    for position, parts in cuts:
        steps = jnp.exp(jax.random.uniform(jax.random.fold_in(own, position), (parts,), jnp.float32, least / len(cuts), top_value / len(cuts)))
        loudness = loudness * jnp.repeat(steps, shape[position] // parts).reshape([-1 if axis == position else 1 for axis in range(len(shape))])
    return loudness


def bell_draw(key, shape, deviation, most, shards=(), kind=jnp.bfloat16):
    result = jax.random.normal(key, shape, jnp.float32) * deviation
    if len(shards) > 0:
        result = shard_levels(key, shape, shards, -0.22, 0.18) * result
    return jnp.clip(result, min=-most, max=most).astype(kind)


def setup_inputs(seed: int = 0) -> dict:
    arg_keys = jax.random.split(jax.random.key(seed), 8)
    energies = jnp.clip(jax.random.uniform(arg_keys[0], (ENERGIES,), jnp.float32, -1.0, 1.0) * shard_levels(arg_keys[0], (ENERGIES,), ((0, 64),), -0.4, 0.0), -1.0, 1.0)
    broadening = jnp.clip(0.3 + 0.7 * jax.random.uniform(arg_keys[1], (ENERGIES,), jnp.float32) ** shard_levels(arg_keys[1], (ENERGIES,), ((0, 64),), -0.2, 0.2), 0.3, 1.0)
    hamiltonian = draw_hamiltonian(jax.random.fold_in(arg_keys[7], 71), 0)
    coupling = bell_draw(arg_keys[3], (ORB, B), (11 * B // 4) ** -0.5, 0.21875, ((0, 4),), jnp.float32)
    propagator = bell_draw(arg_keys[4], (2, MODES, ENERGIES, ENERGIES), ENERGIES ** -0.5, 0.75, (), jnp.float32)
    neighbors = draw_neighbors(jax.random.fold_in(arg_keys[7], 71), 0)
    phonon_modes = set_ends(jax.random.randint(arg_keys[6], (ORB, NEIGH), 0, MODES), jax.random.fold_in(arg_keys[6], 1), 0, MODES - 1).astype(jnp.int32)
    return dict(energies=energies, broadening=broadening, hamiltonian=hamiltonian, coupling=coupling, propagator=propagator, neighbors=neighbors, phonon_modes=phonon_modes)


HIGHEST = lax.Precision.HIGHEST

def complex_product(left, right):
    left_real, left_imag = (left[:, 0], left[:, 1])
    right_real, right_imag = (right[:, 0], right[:, 1])
    first = jnp.matmul(left_real, right_real, precision=HIGHEST)
    second = jnp.matmul(left_imag, right_imag, precision=HIGHEST)
    mixed = jnp.matmul(left_real + left_imag, right_real + right_imag, precision=HIGHEST)
    return jnp.stack([first - second, mixed - first - second], axis=1)

def newton_step(schur, inverse):
    identity = jnp.eye(schur.shape[-1], dtype=jnp.float32)
    residue = -complex_product(schur, inverse)
    residue = residue.at[:, 0].add(2.0 * identity)
    return complex_product(inverse, residue)

def jacobi_refine(schur):
    identity = jnp.eye(schur.shape[-1], dtype=jnp.float32)
    diagonal = jnp.diagonal(schur, axis1=2, axis2=3)
    diag_real, diag_imag = (diagonal[:, 0], diagonal[:, 1])
    modulus = diag_real * diag_real + diag_imag * diag_imag
    inv_real = diag_real / modulus
    inv_imag = -diag_imag / modulus
    outer_real = inv_real[:, :, None] * inv_real[:, None, :] - inv_imag[:, :, None] * inv_imag[:, None, :]
    outer_imag = inv_real[:, :, None] * inv_imag[:, None, :] + inv_imag[:, :, None] * inv_real[:, None, :]
    schur_real, schur_imag = (schur[:, 0], schur[:, 1])
    first_real = 2.0 * identity * inv_real[:, :, None] - (outer_real * schur_real - outer_imag * schur_imag)
    first_imag = 2.0 * identity * inv_imag[:, :, None] - (outer_real * schur_imag + outer_imag * schur_real)
    first_iterate = jnp.stack([first_real, first_imag], axis=1)
    return newton_step(schur, first_iterate)

def convolve_modes(kernel, values, one_hot):
    spread = one_hot[:, None, None, :] * values[None]
    real_part = jnp.einsum('mef,mfp->ep', kernel[0], spread[:, :, 0], precision=HIGHEST) - jnp.einsum('mef,mfp->ep', kernel[1], spread[:, :, 1], precision=HIGHEST)
    imag_part = jnp.einsum('mef,mfp->ep', kernel[0], spread[:, :, 1], precision=HIGHEST) + jnp.einsum('mef,mfp->ep', kernel[1], spread[:, :, 0], precision=HIGHEST)
    return jnp.stack([real_part, imag_part], axis=1)

def dense_sigma(self_part, block_neighbors):
    orbitals = block_neighbors.shape[0]
    reshaped = self_part.reshape(self_part.shape[0], 2, orbitals, block_neighbors.shape[1])
    row_index = jnp.broadcast_to(jnp.arange(orbitals, dtype=jnp.int32)[:, None], block_neighbors.shape)
    empty = jnp.zeros((self_part.shape[0], 2, orbitals, orbitals), jnp.float32)
    return empty.at[:, :, row_index, block_neighbors].add(reshaped)

def reference(energies, broadening, hamiltonian, coupling, propagator, neighbors, phonon_modes):
    coupling_scale = 2.0 * math.sqrt(B / NEIGH)
    identity = jnp.eye(B, dtype=jnp.float32)
    block_count = ORB // B
    previous = jnp.zeros((ENERGIES, 2, B, B), jnp.float32)
    schurs = []
    inverses = []
    for block in range(block_count):
        rows = slice(block * B, (block + 1) * B)
        block_ham = hamiltonian[rows]
        block_cpl = coupling[rows]
        shifted = jnp.stack([energies[:, None, None] * identity - block_ham[None], broadening[:, None, None] * identity + jnp.zeros_like(block_ham)[None]], axis=1)
        through = jnp.matmul(jnp.matmul(block_cpl, previous, precision=HIGHEST), block_cpl.T, precision=HIGHEST)
        schur = shifted - through
        inverse = jacobi_refine(schur)
        schurs.append(schur)
        inverses.append(inverse)
        previous = inverse
    greens = []
    selves = []
    mode_ids = jnp.arange(MODES, dtype=jnp.int32)
    for block in range(block_count):
        rows = slice(block * B, (block + 1) * B)
        block_nbr = neighbors[rows]
        inverse = inverses[block]
        index = jnp.broadcast_to(block_nbr, inverse.shape[:2] + block_nbr.shape)
        pair_green = jnp.take_along_axis(inverse, index, axis=3).reshape(ENERGIES, 2, B * NEIGH)
        modes_flat = phonon_modes[rows].reshape(-1)
        one_hot = (modes_flat[None, :] == mode_ids[:, None]).astype(jnp.float32)
        self_part = coupling_scale * convolve_modes(propagator, pair_green, one_hot)
        sigma = dense_sigma(self_part, block_nbr)
        residue = -complex_product(schurs[block] - sigma, inverse)
        residue = residue.at[:, 0].add(2.0 * identity)
        greens.append(complex_product(inverse, residue))
        selves.append(self_part)
    return (jnp.concatenate(greens, axis=2), jnp.concatenate(selves, axis=2))
```

```python
import functools
import math

import jax
import jax.numpy as jnp
from jax import lax
from jax.experimental import pallas as pl
from jax.experimental.pallas import tpu as pltpu
from jax.sharding import Mesh
from jax.sharding import PartitionSpec as P

B = 256
HALF = B // 2
NEIGH = 32
ENERGY = ("y", "z", "core")
PACKED_H = HALF + 16
PAYLOAD = PACKED_H + B
PIECE = PAYLOAD // 2
GROUPS = 4
ROWS = B // GROUPS
F32 = jnp.float32
BF16 = jnp.bfloat16
VMEM = pl.BlockSpec(memory_space=pltpu.VMEM)
SMEM = pl.BlockSpec(memory_space=pltpu.SMEM)


def iota(shape, dim):
    return lax.broadcasted_iota(jnp.int32, shape, dim)


def split(x):
    high = x.astype(BF16)
    return high, (x - high.astype(F32)).astype(BF16)


def left_real(x):
    high, low = split(x)
    return jnp.concatenate([high, high, low], axis=1)


def left_complex(real, imag):
    return jnp.concatenate([left_real(real), left_real(imag)], axis=1)


def right_real(real, imag):
    real_high, real_low = split(real)
    imag_high, imag_low = split(imag)
    high = jnp.concatenate([real_high, imag_high], axis=1)
    low = jnp.concatenate([real_low, imag_low], axis=1)
    return jnp.concatenate([high, low, high], axis=0)


def right_complex(real, imag):
    return jnp.concatenate([right_real(real, imag), right_real(-imag, real)], axis=0)


def product(left, right):
    both = jnp.dot(left, right, preferred_element_type=F32)
    return both[:, :B], both[:, B:]


def pack_body(h_ref, c_ref, head_ref, piece_ref, payload):
    row = iota((HALF, HALF), 0)
    col = iota((HALF, HALF), 1)
    lower = h_ref[HALF:, HALF:]
    payload[:HALF, :HALF] = jnp.where(row <= col, h_ref[:HALF, :HALF], lower)
    payload[:HALF, HALF:] = h_ref[:HALF, HALF:]
    diagonal = jnp.sum(jnp.where(row == col, lower, 0.0), axis=0, keepdims=True)
    payload[HALF:PACKED_H, :HALF] = jnp.broadcast_to(diagonal, (PACKED_H - HALF, HALF))
    payload[HALF:PACKED_H, HALF:] = jnp.zeros((PACKED_H - HALF, HALF), F32)
    payload[PACKED_H:, :] = c_ref[...]
    head_ref[...] = payload[:PACKED_H, :]
    start = pl.multiple_of(lax.axis_index("core") * PIECE, 8)
    piece_ref[...] = payload[pl.ds(start, PIECE), :]


def pack(hamiltonian, coupling):
    return pl.pallas_call(
        pack_body,
        out_shape=(
            jax.ShapeDtypeStruct((PACKED_H, B), F32),
            jax.ShapeDtypeStruct((PIECE, B), F32),
        ),
        in_specs=[VMEM, VMEM],
        out_specs=(VMEM, VMEM),
        scratch_shapes=[pltpu.VMEM((PAYLOAD, B), F32)],
        name="pack",
    )(hamiltonian, coupling)


def unpack_h(packed_ref, h):
    row = iota((HALF, HALF), 0)
    col = iota((HALF, HALF), 1)
    mixed = packed_ref[:HALF, :HALF]
    turned = mixed.T
    across = packed_ref[:HALF, HALF:]
    h[:HALF, :HALF] = jnp.where(row <= col, mixed, turned)
    h[:HALF, HALF:] = across
    h[HALF:, :HALF] = across.T
    last = jnp.where(row > col, mixed, turned)
    diagonal = packed_ref[HALF : HALF + 1, :HALF]
    h[HALF:, HALF:] = jnp.where(row == col, diagonal, last)


def stage_math(stage, e_ref, eta_ref, h, c, g_in, g_out, p_out):
    row = iota((B, B), 0)
    col = iota((B, B), 1)
    on = row == col

    def finish(negated_real, negated_imag):
        full_real = jnp.where(on, e_ref[0], 0.0) - negated_real
        diag_real = jnp.sum(jnp.where(on, full_real, 0.0), axis=0, keepdims=True)
        side_real = jnp.sum(jnp.where(on, full_real, 0.0), axis=1, keepdims=True)
        if negated_imag is None:
            diag_imag = jnp.full((1, B), eta_ref[0], F32)
            side_imag = jnp.full((B, 1), eta_ref[0], F32)
        else:
            full_imag = jnp.where(on, eta_ref[0], 0.0) - negated_imag
            diag_imag = jnp.sum(jnp.where(on, full_imag, 0.0), axis=0, keepdims=True)
            side_imag = jnp.sum(jnp.where(on, full_imag, 0.0), axis=1, keepdims=True)

        def reciprocal(real, imag):
            modulus = real * real + imag * imag
            return real / modulus, -imag / modulus

        row_real, row_imag = reciprocal(diag_real, diag_imag)
        col_real, col_imag = reciprocal(side_real, side_imag)
        n_real = jnp.where(on, 0.0, -negated_real)
        outer_real = col_real * row_real - col_imag * row_imag
        outer_imag = col_real * row_imag + col_imag * row_real
        if negated_imag is None:
            z_real = outer_real * n_real
            z_imag = outer_imag * n_real
            p_real, p_imag = product(left_real(n_real), right_real(z_real, z_imag))
        else:
            n_imag = jnp.where(on, 0.0, -negated_imag)
            z_real = outer_real * n_real - outer_imag * n_imag
            z_imag = outer_real * n_imag + outer_imag * n_real
            p_real, p_imag = product(left_complex(n_real, n_imag), right_complex(z_real, z_imag))
        x_real = jnp.where(on, row_real, 0.0) - z_real
        x_imag = jnp.where(on, row_imag, 0.0) - z_imag
        add_real, add_imag = product(left_complex(x_real, x_imag), right_complex(p_real, p_imag))
        g_out[0] = x_real + add_real
        g_out[1] = x_imag + add_imag
        if p_out is not None:
            p_out[0] = p_real
            p_out[1] = p_imag

    @pl.when(stage == 0)
    def _():
        finish(h[...], None)

    if g_in is not None:

        @pl.when(stage > 0)
        def _():
            c_high, c_low = split(c[...])
            left = jnp.concatenate([c_high, c_high, c_low], axis=1)
            t_real, t_imag = product(left, right_real(g_in[0], g_in[1]))
            through = jnp.concatenate([left_real(t_real), left_real(t_imag)], axis=0)
            right = jnp.concatenate([c_high, c_low, c_high], axis=1)
            u = lax.dot_general(through, right, (((1,), (1,)), ((), ())), preferred_element_type=F32)
            finish(h[...] + u[:B], u[B:])


def first_body(e_ref, eta_ref, head_ref, g_out, h):
    stage = lax.axis_index("slab") - 3

    @pl.when(stage >= 0)
    def _():
        unpack_h(head_ref, h)
        stage_math(stage, e_ref, eta_ref, h, None, None, g_out, None)


def middle_body(distance, e_ref, eta_ref, mine_ref, other_ref, g_in, g_out, payload, h):
    stage = lax.axis_index("slab") - distance

    @pl.when(stage >= 0)
    def _():
        core = lax.axis_index("core")
        payload[pl.ds(pl.multiple_of(core * PIECE, 8), PIECE), :] = mine_ref[...]
        payload[pl.ds(pl.multiple_of((1 - core) * PIECE, 8), PIECE), :] = other_ref[...]
        unpack_h(payload, h)
        stage_math(stage, e_ref, eta_ref, h, payload.at[PACKED_H:, :], g_in, g_out, None)


def along_lanes(x, index):
    return jnp.take_along_axis(x, index, axis=1)


def last_body(e_ref, eta_ref, h_ref, c_ref, g_in, near_ref, g_out, p_out, pair_out, halves):
    stage_math(lax.axis_index("slab"), e_ref, eta_ref, h_ref, c_ref, g_in, g_out, p_out)
    near = near_ref[...]
    inside = jnp.bitwise_and(near, HALF - 1)
    upper = near >= HALF
    group = iota((ROWS, 128), 1) // NEIGH
    for part in range(2):
        halves[0] = g_out[part, :, :HALF]
        halves[1] = g_out[part, :, HALF:]
        result = jnp.zeros((ROWS, 128), F32)
        for q in range(GROUPS):
            left = halves[0, pl.ds(q, ROWS, stride=GROUPS), :]
            right = halves[1, pl.ds(q, ROWS, stride=GROUPS), :]
            picked = jnp.where(upper, along_lanes(right, inside), along_lanes(left, inside))
            result = jnp.where(group == q, picked, result)
        pair_out[:, part, :] = result


G_SHAPE = jax.ShapeDtypeStruct((2, B, B), F32)


def first(e, eta, head):
    return pl.pallas_call(
        first_body,
        out_shape=G_SHAPE,
        in_specs=[SMEM, SMEM, VMEM],
        out_specs=VMEM,
        scratch_shapes=[pltpu.VMEM((B, B), F32)],
        name="first",
    )(e, eta, head)


def middle(distance, e, eta, mine, other, g):
    return pl.pallas_call(
        functools.partial(middle_body, distance),
        out_shape=G_SHAPE,
        in_specs=[SMEM, SMEM, VMEM, VMEM, VMEM],
        out_specs=VMEM,
        scratch_shapes=[pltpu.VMEM((PAYLOAD, B), F32), pltpu.VMEM((B, B), F32)],
        name="middle",
    )(e, eta, mine, other, g)


def last(e, eta, hamiltonian, coupling, g, near):
    return pl.pallas_call(
        last_body,
        out_shape=(G_SHAPE, G_SHAPE, jax.ShapeDtypeStruct((ROWS, 2, 128), F32)),
        in_specs=[SMEM, SMEM, VMEM, VMEM, VMEM, VMEM],
        out_specs=(VMEM, VMEM, VMEM),
        scratch_shapes=[pltpu.VMEM((2, B, HALF), F32)],
        name="last",
    )(e, eta, hamiltonian, coupling, g, near)


def tables_body(near_ref, mode_ref, d_ref, near_out, mode_out, inverse_out, next_out, rounds_out, weight_out, wide):
    wide[0, :, :NEIGH] = near_ref[...]
    wide[1, :, :NEIGH] = mode_ref[...]
    near_parts, mode_parts = (
        [wide[w, pl.ds(q, ROWS, stride=GROUPS), :][:, :NEIGH] for q in range(GROUPS)] for w in range(2)
    )
    near = jnp.concatenate(near_parts, axis=1)
    near_out[...] = near
    modes = jnp.concatenate(mode_parts, axis=1)
    y, z, core = (lax.axis_index(a) for a in ENERGY)
    mine = (y * lax.axis_size("z") + z) * lax.axis_size("core") + core
    own = jnp.where(iota((ROWS, 128), 0) == mine, modes, 0)
    mode_out[...] = jnp.broadcast_to(jnp.sum(own, axis=0, keepdims=True), (8, 128))
    column = iota((ROWS, B), 1)
    for q in range(GROUPS):
        table = jnp.full((ROWS, B), -1, jnp.int32)
        for k in reversed(range(NEIGH)):
            table = jnp.where(near_parts[q][:, k : k + 1] == column, q * NEIGH + k, table)
        inverse_out[q * ROWS : (q + 1) * ROWS, :] = table
    lane = iota((ROWS, 128), 1)
    place = jnp.bitwise_and(lane, NEIGH - 1)
    follower = jnp.full((ROWS, 128), -1, jnp.int32)
    count = jnp.zeros((ROWS, 128), F32)
    for shift in reversed(range(1, NEIGH)):
        same = (pltpu.roll(near, 128 - shift, axis=1) == near) & (place + shift < NEIGH)
        follower = jnp.where(same, lane + shift, follower)
        count = count + jnp.where(same, 1.0, 0.0)
    next_out[...] = follower
    rounds_out[0] = jnp.max(count).astype(jnp.int32)
    scale = 2.0 * math.sqrt(B / NEIGH)
    modes_count, energies = d_ref.shape[1], d_ref.shape[2]
    size = 2 * energies
    total = modes_count * size
    for m in range(modes_count):
        real = scale * d_ref[0, m]
        imag = scale * d_ref[1, m]
        top = jnp.concatenate([real, -imag], axis=1)
        bottom = jnp.concatenate([imag, real], axis=1)
        high, low = split(jnp.concatenate([top, bottom], axis=0))
        weight_out[:, m * size : (m + 1) * size] = high
        weight_out[:, total + m * size : total + (m + 1) * size] = high
        weight_out[:, 2 * total + m * size : 2 * total + (m + 1) * size] = low


def tables(neighbors, phonon_modes, propagator):
    modes_count, energies = propagator.shape[1:3]
    return pl.pallas_call(
        tables_body,
        out_shape=(
            jax.ShapeDtypeStruct((ROWS, 128), jnp.int32),
            jax.ShapeDtypeStruct((8, 128), jnp.int32),
            jax.ShapeDtypeStruct((B, B), jnp.int32),
            jax.ShapeDtypeStruct((ROWS, 128), jnp.int32),
            jax.ShapeDtypeStruct((1,), jnp.int32),
            jax.ShapeDtypeStruct((2 * energies, 6 * modes_count * energies), BF16),
        ),
        in_specs=[VMEM, VMEM, VMEM],
        out_specs=(VMEM, VMEM, VMEM, VMEM, SMEM, VMEM),
        scratch_shapes=[pltpu.VMEM((2, B, 128), jnp.int32)],
        name="tables",
    )(neighbors, phonon_modes, propagator)


def convolve_body(modes_count, weight_ref, mode_ref, green_ref, out_ref):
    stacked = jnp.concatenate([green_ref[:, 0, :], green_ref[:, 1, :]], axis=0)
    high, low = (x.astype(F32) for x in split(stacked))
    mode = mode_ref[0:1, :]
    highs, lows = [], []
    for m in range(modes_count):
        highs.append(jnp.where(mode == m, high, 0.0).astype(BF16))
        lows.append(jnp.where(mode == m, low, 0.0).astype(BF16))
    right = jnp.concatenate(highs + lows + highs, axis=0)
    result = jnp.dot(weight_ref[...], right, preferred_element_type=F32)
    energies = green_ref.shape[0]
    out_ref[:, 0, :] = result[:energies]
    out_ref[:, 1, :] = result[energies:]


def convolve(modes_count, weight, mode, green):
    return pl.pallas_call(
        functools.partial(convolve_body, modes_count),
        out_shape=jax.ShapeDtypeStruct(green.shape, F32),
        in_specs=[VMEM, VMEM, VMEM],
        out_specs=VMEM,
        name="convolve",
    )(weight, mode, green)


def correct_body(rounds_ref, self_ref, next_ref, inverse_ref, g_ref, p_ref, out_ref, moved):
    part_real = self_ref[:, 0, :]
    part_imag = self_ref[:, 1, :]
    follower = next_ref[...]

    def gather_round(_, carry):
        sum_real, sum_imag, pointer = carry
        valid = pointer >= 0
        index = jnp.maximum(pointer, 0)
        sum_real = sum_real + jnp.where(valid, along_lanes(part_real, index), 0.0)
        sum_imag = sum_imag + jnp.where(valid, along_lanes(part_imag, index), 0.0)
        return sum_real, sum_imag, jnp.where(valid, along_lanes(follower, index), -1)

    sum_real, sum_imag, _ = lax.fori_loop(
        0, rounds_ref[0], gather_round, (part_real, part_imag, follower)
    )
    reals, imags = [], []
    for q in range(GROUPS):
        row_real, row_imag = [], []
        for side in range(2):
            table = inverse_ref[q * ROWS : (q + 1) * ROWS, side * HALF : (side + 1) * HALF]
            valid = table >= 0
            index = jnp.maximum(table, 0)
            row_real.append(jnp.where(valid, along_lanes(sum_real, index), 0.0))
            row_imag.append(jnp.where(valid, along_lanes(sum_imag, index), 0.0))
        reals.append(jnp.concatenate(row_real, axis=1))
        imags.append(jnp.concatenate(row_imag, axis=1))
    sigma_real = jnp.concatenate(reals, axis=0)
    sigma_imag = jnp.concatenate(imags, axis=0)
    g_real, g_imag = g_ref[0], g_ref[1]
    s_real, s_imag = product(left_complex(sigma_real, sigma_imag), right_complex(g_real, g_imag))
    for q in range(GROUPS):
        rows = slice(q * ROWS, (q + 1) * ROWS)
        for part, value in enumerate((s_real, s_imag)):
            for side in range(2):
                piece = value[rows, side * HALF : (side + 1) * HALF]
                moved[2 * part + side, pl.ds(q, ROWS, stride=GROUPS), :] = piece
    moved_real = jnp.concatenate([moved[0], moved[1]], axis=1)
    moved_imag = jnp.concatenate([moved[2], moved[3]], axis=1)
    p_real, p_imag = p_ref[0], p_ref[1]
    square_real, square_imag = product(left_complex(p_real, p_imag), right_complex(p_real, p_imag))
    add_real, add_imag = product(
        left_complex(g_real, g_imag),
        right_complex(square_real + moved_real, square_imag + moved_imag),
    )
    out_ref[0, 0] = g_real + add_real
    out_ref[0, 1] = g_imag + add_imag


def correct(rounds, self_part, follower, inverse, g, p):
    return pl.pallas_call(
        correct_body,
        out_shape=jax.ShapeDtypeStruct((1, 2, B, B), F32),
        in_specs=[SMEM, VMEM, VMEM, VMEM, VMEM, VMEM],
        out_specs=VMEM,
        scratch_shapes=[pltpu.VMEM((4, B, HALF), F32)],
        name="correct",
    )(rounds, self_part, follower, inverse, g, p)


def body(energies, broadening, hamiltonian, coupling, propagator, neighbors, phonon_modes):
    swap = [(0, 1), (1, 0)]
    head, piece = pack(hamiltonian, coupling)
    head0 = lax.ppermute(head, "slab", [(0, 3)])
    far = lax.ppermute(piece, "slab", [(0, 2), (1, 3)])
    near_piece = lax.ppermute(piece, "slab", [(0, 1), (1, 2), (2, 3)])
    far_other = lax.ppermute(far, "core", swap)
    near_other = lax.ppermute(near_piece, "core", swap)
    near, mode, inverse, follower, rounds, weight = tables(neighbors, phonon_modes, propagator)
    g = first(energies, broadening, head0)
    g = middle(2, energies, broadening, far, far_other, g)
    g = middle(1, energies, broadening, near_piece, near_other, g)
    g, p, pairs = last(energies, broadening, hamiltonian, coupling, g, near)
    regrouped = lax.all_to_all(pairs, ENERGY, 0, 0, tiled=True)
    owned = convolve(propagator.shape[1], weight, mode, regrouped)
    returned = lax.all_to_all(owned, ENERGY, 0, 0, tiled=True)
    green = correct(rounds, returned, follower, inverse, g, p)
    self_part = jnp.swapaxes(returned, 0, 1).reshape(1, 2, B * NEIGH)
    return green, self_part


def solution(mesh):
    finer = Mesh(mesh.devices.reshape(mesh.shape["slab"], 4, 8, 2), ("slab", *ENERGY))
    in_specs = (
        P(ENERGY),
        P(ENERGY),
        P("slab", None),
        P("slab", None),
        P(),
        P("slab", None),
        P("slab", None),
    )
    out_specs = (P(ENERGY, None, "slab", None), P(ENERGY, None, "slab"))
    return jax.shard_map(body, mesh=finer, in_specs=in_specs, out_specs=out_specs, check_vma=False)
```

```python
import functools
import math

import jax
import jax.numpy as jnp
from jax import lax
from jax.experimental import pallas as pl
from jax.experimental.pallas import tpu as pltpu
from jax.sharding import Mesh
from jax.sharding import PartitionSpec as P


B = 256
HALF = B // 2
NEIGH = 32
ENERGY = ("y", "z", "core")
PACKED_H = HALF + 16
PAYLOAD = PACKED_H + B
PIECE = PAYLOAD // 2
GROUPS = 4
ROWS = B // GROUPS
F32 = jnp.float32
BF16 = jnp.bfloat16
VMEM = pl.BlockSpec(memory_space=pltpu.VMEM)
SMEM = pl.BlockSpec(memory_space=pltpu.SMEM)
PARAMS = pltpu.CompilerParams(vmem_limit_bytes=16 * 1024 * 1024)


def iota(shape, dim):
    return lax.broadcasted_iota(jnp.int32, shape, dim)


def split(x):
    high = x.astype(BF16)
    return high, (x - high.astype(F32)).astype(BF16)


def left_real(x):
    high, low = split(x)
    return jnp.concatenate([high, high, low], axis=1)


def left_complex(real, imag):
    return jnp.concatenate([left_real(real), left_real(imag)], axis=1)


def right_real(real, imag):
    real_high, real_low = split(real)
    imag_high, imag_low = split(imag)
    high = jnp.concatenate([real_high, imag_high], axis=1)
    low = jnp.concatenate([real_low, imag_low], axis=1)
    return jnp.concatenate([high, low, high], axis=0)


def right_complex(real, imag):
    return jnp.concatenate([right_real(real, imag), right_real(-imag, real)], axis=0)


def product(left, right):
    both = jnp.dot(left, right, preferred_element_type=F32)
    return both[:, :B], both[:, B:]


def pack_body(h_ref, c_ref, head_ref, piece_ref, payload):
    row = iota((HALF, HALF), 0)
    col = iota((HALF, HALF), 1)
    lower = h_ref[HALF:, HALF:]
    payload[:HALF, :HALF] = jnp.where(row <= col, h_ref[:HALF, :HALF], lower)
    payload[:HALF, HALF:] = h_ref[:HALF, HALF:]
    diagonal = jnp.sum(jnp.where(row == col, lower, 0.0), axis=0, keepdims=True)
    payload[HALF:PACKED_H, :HALF] = jnp.broadcast_to(diagonal, (PACKED_H - HALF, HALF))
    payload[HALF:PACKED_H, HALF:] = jnp.zeros((PACKED_H - HALF, HALF), F32)
    payload[PACKED_H:, :] = c_ref[...]
    head_ref[...] = payload[:PACKED_H, :]
    start = pl.multiple_of(lax.axis_index("core") * PIECE, 8)
    piece_ref[...] = payload[pl.ds(start, PIECE), :]


def pack(hamiltonian, coupling):
    return pl.pallas_call(
        pack_body,
        out_shape=(
            jax.ShapeDtypeStruct((PACKED_H, B), F32),
            jax.ShapeDtypeStruct((PIECE, B), F32),
        ),
        in_specs=[VMEM, VMEM],
        out_specs=(VMEM, VMEM),
        scratch_shapes=[pltpu.VMEM((PAYLOAD, B), F32)],
        name="pack",
    )(hamiltonian, coupling)


def unpack_h(packed_ref, h):
    row = iota((HALF, HALF), 0)
    col = iota((HALF, HALF), 1)
    mixed = packed_ref[:HALF, :HALF]
    turned = mixed.T
    across = packed_ref[:HALF, HALF:]
    h[:HALF, :HALF] = jnp.where(row <= col, mixed, turned)
    h[:HALF, HALF:] = across
    h[HALF:, :HALF] = across.T
    last = jnp.where(row > col, mixed, turned)
    diagonal = packed_ref[HALF : HALF + 1, :HALF]
    h[HALF:, HALF:] = jnp.where(row == col, diagonal, last)


def stage_math(stage, e_ref, eta_ref, h, c, g_in, g_out, p_out):
    row = iota((B, B), 0)
    col = iota((B, B), 1)
    on = row == col

    def finish(negated_real, negated_imag):
        full_real = jnp.where(on, e_ref[0], 0.0) - negated_real
        diag_real = jnp.sum(jnp.where(on, full_real, 0.0), axis=0, keepdims=True)
        side_real = jnp.sum(jnp.where(on, full_real, 0.0), axis=1, keepdims=True)
        if negated_imag is None:
            diag_imag = jnp.full((1, B), eta_ref[0], F32)
            side_imag = jnp.full((B, 1), eta_ref[0], F32)
        else:
            full_imag = jnp.where(on, eta_ref[0], 0.0) - negated_imag
            diag_imag = jnp.sum(jnp.where(on, full_imag, 0.0), axis=0, keepdims=True)
            side_imag = jnp.sum(jnp.where(on, full_imag, 0.0), axis=1, keepdims=True)

        def reciprocal(real, imag):
            modulus = real * real + imag * imag
            return real / modulus, -imag / modulus

        row_real, row_imag = reciprocal(diag_real, diag_imag)
        col_real, col_imag = reciprocal(side_real, side_imag)
        n_real = jnp.where(on, 0.0, -negated_real)
        outer_real = col_real * row_real - col_imag * row_imag
        outer_imag = col_real * row_imag + col_imag * row_real
        if negated_imag is None:
            z_real = outer_real * n_real
            z_imag = outer_imag * n_real
            p_real, p_imag = product(left_real(n_real), right_real(z_real, z_imag))
        else:
            n_imag = jnp.where(on, 0.0, -negated_imag)
            z_real = outer_real * n_real - outer_imag * n_imag
            z_imag = outer_real * n_imag + outer_imag * n_real
            p_real, p_imag = product(left_complex(n_real, n_imag), right_complex(z_real, z_imag))
        x_real = jnp.where(on, row_real, 0.0) - z_real
        x_imag = jnp.where(on, row_imag, 0.0) - z_imag
        add_real, add_imag = product(left_complex(x_real, x_imag), right_complex(p_real, p_imag))
        g_out[0] = x_real + add_real
        g_out[1] = x_imag + add_imag
        if p_out is not None:
            p_out[0] = p_real
            p_out[1] = p_imag

    @pl.when(stage == 0)
    def _():
        finish(h[...], None)

    if g_in is not None:

        @pl.when(stage > 0)
        def _():
            c_high, c_low = split(c[...])
            left = jnp.concatenate([c_high, c_high, c_low], axis=1)
            t_real, t_imag = product(left, right_real(g_in[0], g_in[1]))
            through = jnp.concatenate([left_real(t_real), left_real(t_imag)], axis=0)
            right = jnp.concatenate([c_high, c_low, c_high], axis=1)
            u = lax.dot_general(through, right, (((1,), (1,)), ((), ())), preferred_element_type=F32)
            finish(h[...] + u[:B], u[B:])


def first_body(e_ref, eta_ref, head_ref, g_out, h):
    stage = lax.axis_index("slab") - 3

    @pl.when(stage >= 0)
    def _():
        unpack_h(head_ref, h)
        stage_math(stage, e_ref, eta_ref, h, None, None, g_out, None)


def middle_body(distance, e_ref, eta_ref, mine_ref, other_ref, g_in, g_out, payload, h):
    stage = lax.axis_index("slab") - distance

    @pl.when(stage >= 0)
    def _():
        core = lax.axis_index("core")
        payload[pl.ds(pl.multiple_of(core * PIECE, 8), PIECE), :] = mine_ref[...]
        payload[pl.ds(pl.multiple_of((1 - core) * PIECE, 8), PIECE), :] = other_ref[...]
        unpack_h(payload, h)
        stage_math(stage, e_ref, eta_ref, h, payload.at[PACKED_H:, :], g_in, g_out, None)


def along_lanes(x, index):
    return jnp.take_along_axis(x, index, axis=1)


def last_body(e_ref, eta_ref, h_ref, c_ref, g_in, near_ref, g_out, p_out, pair_out, halves):
    stage_math(lax.axis_index("slab"), e_ref, eta_ref, h_ref, c_ref, g_in, g_out, p_out)
    near = near_ref[...]
    inside = jnp.bitwise_and(near, HALF - 1)
    upper = near >= HALF
    group = iota((ROWS, 128), 1) // NEIGH
    for part in range(2):
        halves[0] = g_out[part, :, :HALF]
        halves[1] = g_out[part, :, HALF:]
        result = jnp.zeros((ROWS, 128), F32)
        for q in range(GROUPS):
            left = halves[0, pl.ds(q, ROWS, stride=GROUPS), :]
            right = halves[1, pl.ds(q, ROWS, stride=GROUPS), :]
            picked = jnp.where(upper, along_lanes(right, inside), along_lanes(left, inside))
            result = jnp.where(group == q, picked, result)
        pair_out[:, part, :] = result


G_SHAPE = jax.ShapeDtypeStruct((2, B, B), F32)


def first(e, eta, head):
    return pl.pallas_call(
        first_body,
        out_shape=G_SHAPE,
        in_specs=[SMEM, SMEM, VMEM],
        out_specs=VMEM,
        scratch_shapes=[pltpu.VMEM((B, B), F32)],
        compiler_params=PARAMS,
        name="first",
    )(e, eta, head)


def middle(distance, e, eta, mine, other, g):
    return pl.pallas_call(
        functools.partial(middle_body, distance),
        out_shape=G_SHAPE,
        in_specs=[SMEM, SMEM, VMEM, VMEM, VMEM],
        out_specs=VMEM,
        scratch_shapes=[pltpu.VMEM((PAYLOAD, B), F32), pltpu.VMEM((B, B), F32)],
        compiler_params=PARAMS,
        name="middle",
    )(e, eta, mine, other, g)


def last(e, eta, hamiltonian, coupling, g, near):
    return pl.pallas_call(
        last_body,
        out_shape=(G_SHAPE, G_SHAPE, jax.ShapeDtypeStruct((ROWS, 2, 128), F32)),
        in_specs=[SMEM, SMEM, VMEM, VMEM, VMEM, VMEM],
        out_specs=(VMEM, VMEM, VMEM),
        scratch_shapes=[pltpu.VMEM((2, B, HALF), F32)],
        compiler_params=PARAMS,
        name="last",
    )(e, eta, hamiltonian, coupling, g, near)


def tables_body(near_ref, mode_ref, d_ref, near_out, mode_out, inverse_out, next_out, rounds_out, weight_out, wide):
    wide[0, :, :NEIGH] = near_ref[...].T
    wide[1, :, :NEIGH] = mode_ref[...].T
    near_parts, mode_parts = (
        [wide[w, pl.ds(q, ROWS, stride=GROUPS), :][:, :NEIGH] for q in range(GROUPS)] for w in range(2)
    )
    near = jnp.concatenate(near_parts, axis=1)
    near_out[...] = near
    modes = jnp.concatenate(mode_parts, axis=1)
    y, z, core = (lax.axis_index(a) for a in ENERGY)
    mine = (y * lax.axis_size("z") + z) * lax.axis_size("core") + core
    own = jnp.where(iota((ROWS, 128), 0) == mine, modes, 0)
    mode_out[...] = jnp.broadcast_to(jnp.sum(own, axis=0, keepdims=True), (8, 128))
    column = iota((ROWS, B), 1)
    for q in range(GROUPS):
        table = jnp.full((ROWS, B), -1, jnp.int32)
        for k in reversed(range(NEIGH)):
            table = jnp.where(near_parts[q][:, k : k + 1] == column, q * NEIGH + k, table)
        inverse_out[q * ROWS : (q + 1) * ROWS, :] = table
    lane = iota((ROWS, 128), 1)
    place = jnp.bitwise_and(lane, NEIGH - 1)
    follower = jnp.full((ROWS, 128), -1, jnp.int32)
    count = jnp.zeros((ROWS, 128), F32)
    for shift in reversed(range(1, NEIGH)):
        same = (pltpu.roll(near, 128 - shift, axis=1) == near) & (place + shift < NEIGH)
        follower = jnp.where(same, lane + shift, follower)
        count = count + jnp.where(same, 1.0, 0.0)
    next_out[...] = follower
    rounds_out[0] = jnp.max(count).astype(jnp.int32)
    scale = 2.0 * math.sqrt(B / NEIGH)
    modes_count, energies = d_ref.shape[1], d_ref.shape[2]
    size = 2 * energies
    total = modes_count * size
    for m in range(modes_count):
        real = scale * d_ref[0, m]
        imag = scale * d_ref[1, m]
        top = jnp.concatenate([real, -imag], axis=1)
        bottom = jnp.concatenate([imag, real], axis=1)
        high, low = split(jnp.concatenate([top, bottom], axis=0))
        weight_out[:, m * size : (m + 1) * size] = high
        weight_out[:, total + m * size : total + (m + 1) * size] = high
        weight_out[:, 2 * total + m * size : 2 * total + (m + 1) * size] = low


def tables(neighbors, phonon_modes, propagator):
    modes_count, energies = propagator.shape[1:3]
    return pl.pallas_call(
        tables_body,
        out_shape=(
            jax.ShapeDtypeStruct((ROWS, 128), jnp.int32),
            jax.ShapeDtypeStruct((8, 128), jnp.int32),
            jax.ShapeDtypeStruct((B, B), jnp.int32),
            jax.ShapeDtypeStruct((ROWS, 128), jnp.int32),
            jax.ShapeDtypeStruct((1,), jnp.int32),
            jax.ShapeDtypeStruct((2 * energies, 6 * modes_count * energies), BF16),
        ),
        in_specs=[VMEM, VMEM, VMEM],
        out_specs=(VMEM, VMEM, VMEM, VMEM, SMEM, VMEM),
        scratch_shapes=[pltpu.VMEM((2, B, 128), jnp.int32)],
        compiler_params=PARAMS,
        name="tables",
    )(neighbors, phonon_modes, propagator)


def convolve_body(modes_count, weight_ref, mode_ref, green_ref, out_ref):
    stacked = jnp.concatenate([green_ref[:, 0, :], green_ref[:, 1, :]], axis=0)
    high, low = (x.astype(F32) for x in split(stacked))
    mode = mode_ref[0:1, :]
    highs, lows = [], []
    for m in range(modes_count):
        highs.append(jnp.where(mode == m, high, 0.0).astype(BF16))
        lows.append(jnp.where(mode == m, low, 0.0).astype(BF16))
    right = jnp.concatenate(highs + lows + highs, axis=0)
    result = jnp.dot(weight_ref[...], right, preferred_element_type=F32)
    energies = green_ref.shape[0]
    out_ref[:, 0, :] = result[:energies]
    out_ref[:, 1, :] = result[energies:]


def convolve(modes_count, weight, mode, green):
    return pl.pallas_call(
        functools.partial(convolve_body, modes_count),
        out_shape=jax.ShapeDtypeStruct(green.shape, F32),
        in_specs=[VMEM, VMEM, VMEM],
        out_specs=VMEM,
        compiler_params=PARAMS,
        name="convolve",
    )(weight, mode, green)


def correct_body(rounds_ref, self_ref, next_ref, inverse_ref, g_ref, p_ref, out_ref, self_out, moved):
    self_out[...] = self_ref[...]
    part_real = self_ref[:, 0, :]
    part_imag = self_ref[:, 1, :]
    follower = next_ref[...]

    def gather_round(_, carry):
        sum_real, sum_imag, pointer = carry
        valid = pointer >= 0
        index = jnp.maximum(pointer, 0)
        sum_real = sum_real + jnp.where(valid, along_lanes(part_real, index), 0.0)
        sum_imag = sum_imag + jnp.where(valid, along_lanes(part_imag, index), 0.0)
        return sum_real, sum_imag, jnp.where(valid, along_lanes(follower, index), -1)

    sum_real, sum_imag, _ = lax.fori_loop(
        0, rounds_ref[0], gather_round, (part_real, part_imag, follower)
    )
    reals, imags = [], []
    for q in range(GROUPS):
        row_real, row_imag = [], []
        for side in range(2):
            table = inverse_ref[q * ROWS : (q + 1) * ROWS, side * HALF : (side + 1) * HALF]
            valid = table >= 0
            index = jnp.maximum(table, 0)
            row_real.append(jnp.where(valid, along_lanes(sum_real, index), 0.0))
            row_imag.append(jnp.where(valid, along_lanes(sum_imag, index), 0.0))
        reals.append(jnp.concatenate(row_real, axis=1))
        imags.append(jnp.concatenate(row_imag, axis=1))
    sigma_real = jnp.concatenate(reals, axis=0)
    sigma_imag = jnp.concatenate(imags, axis=0)
    g_real, g_imag = g_ref[0], g_ref[1]
    s_real, s_imag = product(left_complex(sigma_real, sigma_imag), right_complex(g_real, g_imag))
    for q in range(GROUPS):
        rows = slice(q * ROWS, (q + 1) * ROWS)
        for part, value in enumerate((s_real, s_imag)):
            for side in range(2):
                piece = value[rows, side * HALF : (side + 1) * HALF]
                moved[2 * part + side, pl.ds(q, ROWS, stride=GROUPS), :] = piece
    moved_real = jnp.concatenate([moved[0], moved[1]], axis=1)
    moved_imag = jnp.concatenate([moved[2], moved[3]], axis=1)
    p_real, p_imag = p_ref[0], p_ref[1]
    square_real, square_imag = product(left_complex(p_real, p_imag), right_complex(p_real, p_imag))
    add_real, add_imag = product(
        left_complex(g_real, g_imag),
        right_complex(square_real + moved_real, square_imag + moved_imag),
    )
    out_ref[0, 0] = g_real + add_real
    out_ref[0, 1] = g_imag + add_imag


def correct(rounds, self_part, follower, inverse, g, p):
    return pl.pallas_call(
        correct_body,
        out_shape=(
            jax.ShapeDtypeStruct((1, 2, B, B), F32),
            jax.ShapeDtypeStruct(self_part.shape, F32),
        ),
        in_specs=[SMEM, VMEM, VMEM, VMEM, VMEM, VMEM],
        out_specs=(VMEM, VMEM),
        scratch_shapes=[pltpu.VMEM((4, B, HALF), F32)],
        compiler_params=PARAMS,
        name="correct",
    )(rounds, self_part, follower, inverse, g, p)


def body(energies, broadening, hamiltonian, coupling, propagator, neighbors, phonon_modes):
    swap = [(0, 1), (1, 0)]
    head, piece = pack(hamiltonian, coupling)
    head0 = lax.ppermute(head, "slab", [(0, 3)])
    far = lax.ppermute(piece, "slab", [(0, 2), (1, 3)])
    close = lax.ppermute(piece, "slab", [(0, 1), (1, 2), (2, 3)])
    far_other = lax.ppermute(far, "core", swap)
    close_other = lax.ppermute(close, "core", swap)
    near, mode, inverse, follower, rounds, weight = tables(neighbors.T, phonon_modes.T, propagator)
    g = first(energies, broadening, head0)
    g = middle(2, energies, broadening, far, far_other, g)
    g = middle(1, energies, broadening, close, close_other, g)
    g, p, pairs = last(energies, broadening, hamiltonian, coupling, g, near)
    regrouped = lax.all_to_all(pairs, ENERGY, 0, 0, tiled=True)
    owned = convolve(propagator.shape[1], weight, mode, regrouped)
    returned = lax.all_to_all(owned, ENERGY, 0, 0, tiled=True)
    green, self_part = correct(rounds, returned, follower, inverse, g, p)
    self_part = jnp.swapaxes(self_part, 0, 1).reshape(1, 2, B * NEIGH)
    return green, self_part


def solution(mesh):
    finer = Mesh(mesh.devices.reshape(mesh.shape["slab"], 4, 8, 2), ("slab", *ENERGY))
    in_specs = (
        P(ENERGY),
        P(ENERGY),
        P("slab", None),
        P("slab", None),
        P(),
        P("slab", None),
        P("slab", None),
    )
    out_specs = (P(ENERGY, None, "slab", None), P(ENERGY, None, "slab"))
    return jax.shard_map(body, mesh=finer, in_specs=in_specs, out_specs=out_specs, check_vma=False)
```

```python
import functools
import math

import jax
import jax.numpy as jnp
from jax import lax
from jax.experimental import pallas as pl
from jax.experimental.pallas import tpu as pltpu
from jax.sharding import Mesh
from jax.sharding import PartitionSpec as P


B = 256
HALF = B // 2
NEIGH = 32
ENERGY = ("y", "z", "core")
PACKED_H = HALF + 16
PAYLOAD = PACKED_H + B
PIECE = PAYLOAD // 2
GROUPS = 4
ROWS = B // GROUPS
F32 = jnp.float32
BF16 = jnp.bfloat16
VMEM = pl.BlockSpec(memory_space=pltpu.VMEM)
SMEM = pl.BlockSpec(memory_space=pltpu.SMEM)
HBM = pl.BlockSpec(memory_space=pltpu.HBM)
PARAMS = pltpu.CompilerParams(vmem_limit_bytes=16 * 1024 * 1024)


def iota(shape, dim):
    return lax.broadcasted_iota(jnp.int32, shape, dim)


def split(x):
    high = x.astype(BF16)
    return high, (x - high.astype(F32)).astype(BF16)


def dot(left, right):
    return jnp.dot(left, right, preferred_element_type=F32)


def dot_turned(left, right):
    return lax.dot_general(left, right, (((1,), (1,)), ((), ())), preferred_element_type=F32)


def stacked(real, imag):
    high, low = split(jnp.concatenate([real, imag], axis=0))
    return jnp.concatenate([high, low], axis=0)


def three_passes(left, right_high, right_low, multiply=dot):
    rows = left.shape[0] // 2
    wide = multiply(left, right_high)
    return wide[:rows] + wide[rows:] + multiply(left[:rows], right_low)


def complex_product(left, right):
    size = right.shape[0] // 4
    by_real = three_passes(left, right[:size], right[2 * size : 3 * size])
    by_imag = three_passes(left, right[size : 2 * size], right[3 * size :])
    return by_real[:size] - by_imag[size:], by_real[size:] + by_imag[:size]


def real_product(left, right):
    size = right.shape[0] // 4
    by_real = three_passes(left, right[:size], right[2 * size : 3 * size])
    by_imag = three_passes(left, right[size : 2 * size], right[3 * size :])
    return by_real, by_imag


def pack_body(h_ref, c_ref, head_ref, piece_ref, h, sems):
    core = lax.axis_index("core")
    load = pltpu.make_async_copy(h_ref, h, sems.at[0])
    load.start()
    first_rows = PIECE - PACKED_H
    begin = pltpu.make_async_copy(
        c_ref.at[pl.ds(0, first_rows)], piece_ref.at[pl.ds(PACKED_H, first_rows)], sems.at[1]
    )
    rest = pltpu.make_async_copy(c_ref.at[pl.ds(first_rows, PIECE)], piece_ref, sems.at[1])

    @pl.when(core == 0)
    def _():
        begin.start()

    @pl.when(core != 0)
    def _():
        rest.start()

    load.wait()
    row = iota((HALF, HALF), 0)
    col = iota((HALF, HALF), 1)
    lower = h[HALF:, HALF:]
    head_ref[:HALF, :HALF] = jnp.where(row <= col, h[:HALF, :HALF], lower)
    head_ref[:HALF, HALF:] = h[:HALF, HALF:]
    diagonal = jnp.sum(jnp.where(row == col, lower, 0.0), axis=0, keepdims=True)
    head_ref[HALF:PACKED_H, :HALF] = jnp.broadcast_to(diagonal, (PACKED_H - HALF, HALF))
    head_ref[HALF:PACKED_H, HALF:] = jnp.zeros((PACKED_H - HALF, HALF), F32)

    @pl.when(core == 0)
    def _():
        piece_ref[:PACKED_H, :] = head_ref[...]
        begin.wait()

    @pl.when(core != 0)
    def _():
        rest.wait()


def pack(hamiltonian, coupling):
    return pl.pallas_call(
        pack_body,
        out_shape=(
            jax.ShapeDtypeStruct((PACKED_H, B), F32),
            jax.ShapeDtypeStruct((PIECE, B), F32),
        ),
        in_specs=[HBM, HBM],
        out_specs=(VMEM, VMEM),
        scratch_shapes=[pltpu.VMEM((B, B), F32), pltpu.SemaphoreType.DMA((2,))],
        compiler_params=PARAMS,
        name="pack",
    )(*(pltpu.with_memory_space_constraint(x, pltpu.HBM) for x in (hamiltonian, coupling)))


def unpack_h(packed_ref, h):
    row = iota((HALF, HALF), 0)
    col = iota((HALF, HALF), 1)
    mixed = packed_ref[:HALF, :HALF]
    turned = mixed.T
    across = packed_ref[:HALF, HALF:]
    h[:HALF, :HALF] = jnp.where(row <= col, mixed, turned)
    h[:HALF, HALF:] = across
    h[HALF:, :HALF] = across.T
    last = jnp.where(row > col, mixed, turned)
    diagonal = packed_ref[HALF : HALF + 1, :HALF]
    h[HALF:, HALF:] = jnp.where(row == col, diagonal, last)


def stage_math(stage, e_ref, eta_ref, h, c, g_in, g_out, p_out):
    row = iota((B, B), 0)
    col = iota((B, B), 1)
    on = row == col

    def finish(negated_real, negated_imag):
        full_real = jnp.where(on, e_ref[0], 0.0) - negated_real
        diag_real = jnp.sum(jnp.where(on, full_real, 0.0), axis=0, keepdims=True)
        side_real = jnp.sum(jnp.where(on, full_real, 0.0), axis=1, keepdims=True)
        if negated_imag is None:
            diag_imag = jnp.full((1, B), eta_ref[0], F32)
            side_imag = jnp.full((B, 1), eta_ref[0], F32)
        else:
            full_imag = jnp.where(on, eta_ref[0], 0.0) - negated_imag
            diag_imag = jnp.sum(jnp.where(on, full_imag, 0.0), axis=0, keepdims=True)
            side_imag = jnp.sum(jnp.where(on, full_imag, 0.0), axis=1, keepdims=True)

        def reciprocal(real, imag):
            modulus = real * real + imag * imag
            return real / modulus, -imag / modulus

        row_real, row_imag = reciprocal(diag_real, diag_imag)
        col_real, col_imag = reciprocal(side_real, side_imag)
        n_real = jnp.where(on, 0.0, -negated_real)
        outer_real = col_real * row_real - col_imag * row_imag
        outer_imag = col_real * row_imag + col_imag * row_real
        if negated_imag is None:
            z_real = outer_real * n_real
            z_imag = outer_imag * n_real
            high, low = split(n_real)
            p_real, p_imag = real_product(
                jnp.concatenate([high, low], axis=0), stacked(z_real, z_imag)
            )
        else:
            n_imag = jnp.where(on, 0.0, -negated_imag)
            z_real = outer_real * n_real - outer_imag * n_imag
            z_imag = outer_real * n_imag + outer_imag * n_real
            p_real, p_imag = complex_product(stacked(n_real, n_imag), stacked(z_real, z_imag))
        x_real = jnp.where(on, row_real, 0.0) - z_real
        x_imag = jnp.where(on, row_imag, 0.0) - z_imag
        add_real, add_imag = complex_product(stacked(x_real, x_imag), stacked(p_real, p_imag))
        g_out[0] = x_real + add_real
        g_out[1] = x_imag + add_imag
        if p_out is not None:
            p_out[0] = p_real
            p_out[1] = p_imag

    @pl.when(stage == 0)
    def _():
        finish(h[...], None)

    if g_in is not None:

        @pl.when(stage > 0)
        def _():
            c_high, c_low = split(c[...])
            left = jnp.concatenate([c_high, c_low], axis=0)
            t_real, t_imag = real_product(left, stacked(g_in[0], g_in[1]))
            u = three_passes(stacked(t_real, t_imag), c_high, c_low, dot_turned)
            finish(h[...] + u[:B], u[B:])


def first_body(e_ref, eta_ref, head_ref, g_out, h):
    stage = lax.axis_index("slab") - 3

    @pl.when(stage >= 0)
    def _():
        unpack_h(head_ref, h)
        stage_math(stage, e_ref, eta_ref, h, None, None, g_out, None)


def middle_body(distance, e_ref, eta_ref, mine_ref, other_ref, g_in, g_out, payload, h):
    stage = lax.axis_index("slab") - distance

    @pl.when(stage >= 0)
    def _():
        core = lax.axis_index("core")
        payload[pl.ds(pl.multiple_of(core * PIECE, 8), PIECE), :] = mine_ref[...]
        payload[pl.ds(pl.multiple_of((1 - core) * PIECE, 8), PIECE), :] = other_ref[...]
        unpack_h(payload, h)
        stage_math(stage, e_ref, eta_ref, h, payload.at[PACKED_H:, :], g_in, g_out, None)


def along_lanes(x, index):
    return jnp.take_along_axis(x, index, axis=1)


def last_body(e_ref, eta_ref, h_ref, c_ref, g_in, near_ref, g_out, p_out, pair_out, halves):
    stage_math(lax.axis_index("slab"), e_ref, eta_ref, h_ref, c_ref, g_in, g_out, p_out)
    near = near_ref[...]
    inside = jnp.bitwise_and(near, HALF - 1)
    upper = near >= HALF
    group = iota((ROWS, 128), 1) // NEIGH
    for part in range(2):
        halves[0] = g_out[part, :, :HALF]
        halves[1] = g_out[part, :, HALF:]
        result = jnp.zeros((ROWS, 128), F32)
        for q in range(GROUPS):
            left = halves[0, pl.ds(q, ROWS, stride=GROUPS), :]
            right = halves[1, pl.ds(q, ROWS, stride=GROUPS), :]
            picked = jnp.where(upper, along_lanes(right, inside), along_lanes(left, inside))
            result = jnp.where(group == q, picked, result)
        pair_out[:, part, :] = result


G_SHAPE = jax.ShapeDtypeStruct((2, B, B), F32)


def first(e, eta, head):
    return pl.pallas_call(
        first_body,
        out_shape=G_SHAPE,
        in_specs=[SMEM, SMEM, VMEM],
        out_specs=VMEM,
        scratch_shapes=[pltpu.VMEM((B, B), F32)],
        compiler_params=PARAMS,
        name="first",
    )(e, eta, head)


def middle(distance, e, eta, mine, other, g):
    return pl.pallas_call(
        functools.partial(middle_body, distance),
        out_shape=G_SHAPE,
        in_specs=[SMEM, SMEM, VMEM, VMEM, VMEM],
        out_specs=VMEM,
        scratch_shapes=[pltpu.VMEM((PAYLOAD, B), F32), pltpu.VMEM((B, B), F32)],
        compiler_params=PARAMS,
        name="middle",
    )(e, eta, mine, other, g)


def last(e, eta, hamiltonian, coupling, g, near):
    return pl.pallas_call(
        last_body,
        out_shape=(G_SHAPE, G_SHAPE, jax.ShapeDtypeStruct((ROWS, 2, 128), F32)),
        in_specs=[SMEM, SMEM, VMEM, VMEM, VMEM, VMEM],
        out_specs=(VMEM, VMEM, VMEM),
        scratch_shapes=[pltpu.VMEM((2, B, HALF), F32)],
        compiler_params=PARAMS,
        name="last",
    )(e, eta, hamiltonian, coupling, g, near)


def tables_body(near_ref, mode_ref, d_ref, near_out, mode_out, inverse_out, next_out, rounds_out, weight_out, wide):
    wide[0, :, :NEIGH] = near_ref[...].T
    wide[1, :, :NEIGH] = mode_ref[...].T
    near_parts, mode_parts = (
        [wide[w, pl.ds(q, ROWS, stride=GROUPS), :][:, :NEIGH] for q in range(GROUPS)] for w in range(2)
    )
    near = jnp.concatenate(near_parts, axis=1)
    near_out[...] = near
    modes = jnp.concatenate(mode_parts, axis=1)
    y, z, core = (lax.axis_index(a) for a in ENERGY)
    mine = (y * lax.axis_size("z") + z) * lax.axis_size("core") + core
    own = jnp.where(iota((ROWS, 128), 0) == mine, modes, 0)
    mode_out[...] = jnp.broadcast_to(jnp.sum(own, axis=0, keepdims=True), (8, 128))
    column = iota((ROWS, B), 1)
    for q in range(GROUPS):
        table = jnp.full((ROWS, B), -1, jnp.int32)
        for k in reversed(range(NEIGH)):
            table = jnp.where(near_parts[q][:, k : k + 1] == column, q * NEIGH + k, table)
        inverse_out[q * ROWS : (q + 1) * ROWS, :] = table
    lane = iota((ROWS, 128), 1)
    place = jnp.bitwise_and(lane, NEIGH - 1)
    follower = jnp.full((ROWS, 128), -1, jnp.int32)
    count = jnp.zeros((ROWS, 128), F32)
    for shift in reversed(range(1, NEIGH)):
        same = (pltpu.roll(near, 128 - shift, axis=1) == near) & (place + shift < NEIGH)
        follower = jnp.where(same, lane + shift, follower)
        count = count + jnp.where(same, 1.0, 0.0)
    next_out[...] = follower
    rounds_out[...] = jnp.broadcast_to(jnp.max(count, axis=0, keepdims=True), (8, 128))
    scale = 2.0 * math.sqrt(B / NEIGH)
    modes_count, energies = d_ref.shape[1], d_ref.shape[2]
    size = 2 * energies
    total = modes_count * size
    for m in range(modes_count):
        real = scale * d_ref[0, m]
        imag = scale * d_ref[1, m]
        top = jnp.concatenate([real, -imag], axis=1)
        bottom = jnp.concatenate([imag, real], axis=1)
        high, low = split(jnp.concatenate([top, bottom], axis=0))
        weight_out[:, m * size : (m + 1) * size] = high
        weight_out[:, total + m * size : total + (m + 1) * size] = high
        weight_out[:, 2 * total + m * size : 2 * total + (m + 1) * size] = low


def tables(neighbors, phonon_modes, propagator):
    modes_count, energies = propagator.shape[1:3]
    return pl.pallas_call(
        tables_body,
        out_shape=(
            jax.ShapeDtypeStruct((ROWS, 128), jnp.int32),
            jax.ShapeDtypeStruct((8, 128), jnp.int32),
            jax.ShapeDtypeStruct((B, B), jnp.int32),
            jax.ShapeDtypeStruct((ROWS, 128), jnp.int32),
            jax.ShapeDtypeStruct((8, 128), F32),
            jax.ShapeDtypeStruct((2 * energies, 6 * modes_count * energies), BF16),
        ),
        in_specs=[VMEM, VMEM, VMEM],
        out_specs=(VMEM, VMEM, VMEM, VMEM, VMEM, VMEM),
        scratch_shapes=[pltpu.VMEM((2, B, 128), jnp.int32)],
        compiler_params=PARAMS,
        name="tables",
    )(neighbors, phonon_modes, propagator)


def convolve_body(modes_count, weight_ref, mode_ref, green_ref, out_ref):
    stacked = jnp.concatenate([green_ref[:, 0, :], green_ref[:, 1, :]], axis=0)
    high, low = (x.astype(F32) for x in split(stacked))
    mode = mode_ref[0:1, :]
    highs, lows = [], []
    for m in range(modes_count):
        highs.append(jnp.where(mode == m, high, 0.0).astype(BF16))
        lows.append(jnp.where(mode == m, low, 0.0).astype(BF16))
    right = jnp.concatenate(highs + lows + highs, axis=0)
    result = jnp.dot(weight_ref[...], right, preferred_element_type=F32)
    energies = green_ref.shape[0]
    out_ref[:, 0, :] = result[:energies]
    out_ref[:, 1, :] = result[energies:]


def convolve(modes_count, weight, mode, green):
    return pl.pallas_call(
        functools.partial(convolve_body, modes_count),
        out_shape=jax.ShapeDtypeStruct(green.shape, F32),
        in_specs=[VMEM, VMEM, VMEM],
        out_specs=VMEM,
        compiler_params=PARAMS,
        name="convolve",
    )(weight, mode, green)


def beside_body(g_ref, p_ref, base_out, split_out):
    g_stack = stacked(g_ref[0], g_ref[1])
    split_out[...] = g_stack
    p_stack = stacked(p_ref[0], p_ref[1])
    square_real, square_imag = complex_product(p_stack, p_stack)
    add_real, add_imag = complex_product(g_stack, stacked(square_real, square_imag))
    base_out[0] = g_ref[0] + add_real
    base_out[1] = g_ref[1] + add_imag


def beside(g, p):
    return pl.pallas_call(
        beside_body,
        out_shape=(G_SHAPE, jax.ShapeDtypeStruct((4 * B, B), BF16)),
        in_specs=[VMEM, VMEM],
        out_specs=(VMEM, VMEM),
        compiler_params=PARAMS,
        cost_estimate=pl.CostEstimate(
            flops=2 * 24 * B * B * B, bytes_accessed=6 * 4 * B * B, transcendentals=0
        ),
        name="beside",
    )(g, p)


def correct_body(rounds_ref, self_ref, next_ref, inverse_ref, base_ref, split_ref, out_ref, self_out, moved):
    self_out[...] = self_ref[...]
    part_real = self_ref[:, 0, :]
    part_imag = self_ref[:, 1, :]
    follower = next_ref[...]

    def gather_round(_, carry):
        sum_real, sum_imag, pointer = carry
        valid = pointer >= 0
        index = jnp.maximum(pointer, 0)
        sum_real = sum_real + jnp.where(valid, along_lanes(part_real, index), 0.0)
        sum_imag = sum_imag + jnp.where(valid, along_lanes(part_imag, index), 0.0)
        return sum_real, sum_imag, jnp.where(valid, along_lanes(follower, index), -1)

    sum_real, sum_imag, _ = lax.fori_loop(
        0, jnp.max(rounds_ref[...]).astype(jnp.int32), gather_round, (part_real, part_imag, follower)
    )
    reals, imags = [], []
    for q in range(GROUPS):
        row_real, row_imag = [], []
        for side in range(2):
            table = inverse_ref[q * ROWS : (q + 1) * ROWS, side * HALF : (side + 1) * HALF]
            valid = table >= 0
            index = jnp.maximum(table, 0)
            row_real.append(jnp.where(valid, along_lanes(sum_real, index), 0.0))
            row_imag.append(jnp.where(valid, along_lanes(sum_imag, index), 0.0))
        reals.append(jnp.concatenate(row_real, axis=1))
        imags.append(jnp.concatenate(row_imag, axis=1))
    sigma_real = jnp.concatenate(reals, axis=0)
    sigma_imag = jnp.concatenate(imags, axis=0)
    g_stack = split_ref[...]
    s_real, s_imag = complex_product(stacked(sigma_real, sigma_imag), g_stack)
    for q in range(GROUPS):
        rows = slice(q * ROWS, (q + 1) * ROWS)
        for part, value in enumerate((s_real, s_imag)):
            for side in range(2):
                piece = value[rows, side * HALF : (side + 1) * HALF]
                moved[2 * part + side, pl.ds(q, ROWS, stride=GROUPS), :] = piece
    moved_real = jnp.concatenate([moved[0], moved[1]], axis=1)
    moved_imag = jnp.concatenate([moved[2], moved[3]], axis=1)
    add_real, add_imag = complex_product(g_stack, stacked(moved_real, moved_imag))
    out_ref[0, 0] = base_ref[0] + add_real
    out_ref[0, 1] = base_ref[1] + add_imag


def correct(rounds, self_part, follower, inverse, base, g_split):
    return pl.pallas_call(
        correct_body,
        out_shape=(
            jax.ShapeDtypeStruct((1, 2, B, B), F32),
            jax.ShapeDtypeStruct(self_part.shape, F32),
        ),
        in_specs=[VMEM] * 6,
        out_specs=(VMEM, VMEM),
        scratch_shapes=[pltpu.VMEM((4, B, HALF), F32)],
        compiler_params=PARAMS,
        name="correct",
    )(rounds, self_part, follower, inverse, base, g_split)


def shifted(x, distance):
    count = lax.axis_size("slab")
    return lax.ppermute(x, "slab", [(i, (i + distance) % count) for i in range(count)])


def body(energies, broadening, hamiltonian, coupling, propagator, neighbors, phonon_modes):
    swap = [(0, 1), (1, 0)]
    head, piece = pack(hamiltonian, coupling)
    far = shifted(piece, 2)
    head0 = shifted(head, 3)
    close = shifted(piece, 1)
    far_other = lax.ppermute(far, "core", swap)
    close_other = lax.ppermute(close, "core", swap)
    near, mode, inverse, follower, rounds, weight = tables(neighbors.T, phonon_modes.T, propagator)
    g = first(energies, broadening, head0)
    g = middle(2, energies, broadening, far, far_other, g)
    g = middle(1, energies, broadening, close, close_other, g)
    g, p, pairs = last(energies, broadening, hamiltonian, coupling, g, near)
    regrouped = lax.all_to_all(pairs, ENERGY, 0, 0, tiled=True)
    base, g_split = beside(g, p)
    owned = convolve(propagator.shape[1], weight, mode, regrouped)
    returned = lax.all_to_all(owned, ENERGY, 0, 0, tiled=True)
    green, self_part = correct(rounds, returned, follower, inverse, base, g_split)
    self_part = jnp.swapaxes(self_part, 0, 1).reshape(1, 2, B * NEIGH)
    return green, self_part


def solution(mesh):
    finer = Mesh(mesh.devices.reshape(mesh.shape["slab"], 4, 8, 2), ("slab", *ENERGY))
    in_specs = (
        P(ENERGY),
        P(ENERGY),
        P("slab", None),
        P("slab", None),
        P(),
        P("slab", None),
        P("slab", None),
    )
    out_specs = (P(ENERGY, None, "slab", None), P(ENERGY, None, "slab"))
    return jax.shard_map(body, mesh=finer, in_specs=in_specs, out_specs=out_specs, check_vma=False)
```

```python
import functools
import math

import jax
import jax.numpy as jnp
from jax import lax
from jax.experimental import pallas as pl
from jax.experimental.pallas import tpu as pltpu
from jax.sharding import Mesh
from jax.sharding import PartitionSpec as P


B = 256
HALF = B // 2
NEIGH = 32
ENERGY = ("y", "z", "core")
PACKED_H = HALF + 16
PAYLOAD = PACKED_H + B
PIECE = PAYLOAD // 2
GROUPS = 4
ROWS = B // GROUPS
F32 = jnp.float32
BF16 = jnp.bfloat16
VMEM = pl.BlockSpec(memory_space=pltpu.VMEM)
SMEM = pl.BlockSpec(memory_space=pltpu.SMEM)
HBM = pl.BlockSpec(memory_space=pltpu.HBM)
PARAMS = pltpu.CompilerParams(vmem_limit_bytes=16 * 1024 * 1024)


def iota(shape, dim):
    return lax.broadcasted_iota(jnp.int32, shape, dim)


def split(x):
    high = x.astype(BF16)
    return high, (x - high.astype(F32)).astype(BF16)


def dot(left, right):
    return jnp.dot(left, right, preferred_element_type=F32)


def dot_turned(left, right):
    return lax.dot_general(left, right, (((1,), (1,)), ((), ())), preferred_element_type=F32)


def three_passes(left, right, multiply=dot):
    high, low = left
    return multiply(high, right[0]) + multiply(low, right[0]) + multiply(high, right[1])


def thirds(real, imag):
    return split(real), split(imag), split(real + imag)


def complex_product(left, right):
    first, second, mixed = (three_passes(x, y) for x, y in zip(left, right))
    return first - second, mixed - first - second


def pack_body(h_ref, c_ref, head_ref, piece_ref, h, sems):
    core = lax.axis_index("core")
    load = pltpu.make_async_copy(h_ref, h, sems.at[0])
    load.start()
    first_rows = PIECE - PACKED_H
    begin = pltpu.make_async_copy(
        c_ref.at[pl.ds(0, first_rows)], piece_ref.at[pl.ds(PACKED_H, first_rows)], sems.at[1]
    )
    rest = pltpu.make_async_copy(c_ref.at[pl.ds(first_rows, PIECE)], piece_ref, sems.at[1])

    @pl.when(core == 0)
    def _():
        begin.start()

    @pl.when(core != 0)
    def _():
        rest.start()

    load.wait()
    row = iota((HALF, HALF), 0)
    col = iota((HALF, HALF), 1)
    lower = h[HALF:, HALF:]
    head_ref[:HALF, :HALF] = jnp.where(row <= col, h[:HALF, :HALF], lower)
    head_ref[:HALF, HALF:] = h[:HALF, HALF:]
    diagonal = jnp.sum(jnp.where(row == col, lower, 0.0), axis=0, keepdims=True)
    head_ref[HALF:PACKED_H, :HALF] = jnp.broadcast_to(diagonal, (PACKED_H - HALF, HALF))
    head_ref[HALF:PACKED_H, HALF:] = jnp.zeros((PACKED_H - HALF, HALF), F32)

    @pl.when(core == 0)
    def _():
        piece_ref[:PACKED_H, :] = head_ref[...]
        begin.wait()

    @pl.when(core != 0)
    def _():
        rest.wait()


def pack(hamiltonian, coupling):
    return pl.pallas_call(
        pack_body,
        out_shape=(
            jax.ShapeDtypeStruct((PACKED_H, B), F32),
            jax.ShapeDtypeStruct((PIECE, B), F32),
        ),
        in_specs=[HBM, HBM],
        out_specs=(VMEM, VMEM),
        scratch_shapes=[pltpu.VMEM((B, B), F32), pltpu.SemaphoreType.DMA((2,))],
        compiler_params=PARAMS,
        name="pack",
    )(*(pltpu.with_memory_space_constraint(x, pltpu.HBM) for x in (hamiltonian, coupling)))


def unpack_h(packed_ref, h):
    row = iota((HALF, HALF), 0)
    col = iota((HALF, HALF), 1)
    mixed = packed_ref[:HALF, :HALF]
    turned = mixed.T
    across = packed_ref[:HALF, HALF:]
    h[:HALF, :HALF] = jnp.where(row <= col, mixed, turned)
    h[:HALF, HALF:] = across
    h[HALF:, :HALF] = across.T
    last = jnp.where(row > col, mixed, turned)
    diagonal = packed_ref[HALF : HALF + 1, :HALF]
    h[HALF:, HALF:] = jnp.where(row == col, diagonal, last)


def stage_math(stage, e_ref, eta_ref, h, c, g_in, g_out, p_out):
    row = iota((B, B), 0)
    col = iota((B, B), 1)
    on = row == col

    def finish(negated_real, negated_imag):
        full_real = jnp.where(on, e_ref[0], 0.0) - negated_real
        diag_real = jnp.sum(jnp.where(on, full_real, 0.0), axis=0, keepdims=True)
        side_real = jnp.sum(jnp.where(on, full_real, 0.0), axis=1, keepdims=True)
        if negated_imag is None:
            diag_imag = jnp.full((1, B), eta_ref[0], F32)
            side_imag = jnp.full((B, 1), eta_ref[0], F32)
        else:
            full_imag = jnp.where(on, eta_ref[0], 0.0) - negated_imag
            diag_imag = jnp.sum(jnp.where(on, full_imag, 0.0), axis=0, keepdims=True)
            side_imag = jnp.sum(jnp.where(on, full_imag, 0.0), axis=1, keepdims=True)

        def reciprocal(real, imag):
            modulus = real * real + imag * imag
            return real / modulus, -imag / modulus

        row_real, row_imag = reciprocal(diag_real, diag_imag)
        col_real, col_imag = reciprocal(side_real, side_imag)
        n_real = jnp.where(on, 0.0, -negated_real)
        outer_real = col_real * row_real - col_imag * row_imag
        outer_imag = col_real * row_imag + col_imag * row_real
        if negated_imag is None:
            z_real = outer_real * n_real
            z_imag = outer_imag * n_real
            n_split = split(n_real)
            p_real, p_imag = (three_passes(n_split, split(z)) for z in (z_real, z_imag))
        else:
            n_imag = jnp.where(on, 0.0, -negated_imag)
            z_real = outer_real * n_real - outer_imag * n_imag
            z_imag = outer_real * n_imag + outer_imag * n_real
            p_real, p_imag = complex_product(thirds(n_real, n_imag), thirds(z_real, z_imag))
        x_real = jnp.where(on, row_real, 0.0) - z_real
        x_imag = jnp.where(on, row_imag, 0.0) - z_imag
        add_real, add_imag = complex_product(thirds(x_real, x_imag), thirds(p_real, p_imag))
        g_out[0] = x_real + add_real
        g_out[1] = x_imag + add_imag
        if p_out is not None:
            p_out[0] = p_real
            p_out[1] = p_imag

    @pl.when(stage == 0)
    def _():
        finish(h[...], None)

    if g_in is not None:

        @pl.when(stage > 0)
        def _():
            c_split = split(c[...])
            u_real, u_imag = (
                three_passes(split(three_passes(c_split, split(g_in[part]))), c_split, dot_turned)
                for part in range(2)
            )
            finish(h[...] + u_real, u_imag)


def first_body(e_ref, eta_ref, head_ref, g_out, h):
    stage = lax.axis_index("slab") - 3

    @pl.when(stage >= 0)
    def _():
        unpack_h(head_ref, h)
        stage_math(stage, e_ref, eta_ref, h, None, None, g_out, None)


def middle_body(distance, e_ref, eta_ref, mine_ref, other_ref, g_in, g_out, payload, h):
    stage = lax.axis_index("slab") - distance

    @pl.when(stage >= 0)
    def _():
        core = lax.axis_index("core")
        payload[pl.ds(pl.multiple_of(core * PIECE, 8), PIECE), :] = mine_ref[...]
        payload[pl.ds(pl.multiple_of((1 - core) * PIECE, 8), PIECE), :] = other_ref[...]
        unpack_h(payload, h)
        stage_math(stage, e_ref, eta_ref, h, payload.at[PACKED_H:, :], g_in, g_out, None)


def along_lanes(x, index):
    return jnp.take_along_axis(x, index, axis=1)


def last_body(e_ref, eta_ref, h_ref, c_ref, g_in, near_ref, g_out, p_out, pair_out, halves):
    stage_math(lax.axis_index("slab"), e_ref, eta_ref, h_ref, c_ref, g_in, g_out, p_out)
    near = near_ref[...]
    inside = jnp.bitwise_and(near, HALF - 1)
    upper = near >= HALF
    group = iota((ROWS, 128), 1) // NEIGH
    for part in range(2):
        halves[0] = g_out[part, :, :HALF]
        halves[1] = g_out[part, :, HALF:]
        result = jnp.zeros((ROWS, 128), F32)
        for q in range(GROUPS):
            left = halves[0, pl.ds(q, ROWS, stride=GROUPS), :]
            right = halves[1, pl.ds(q, ROWS, stride=GROUPS), :]
            picked = jnp.where(upper, along_lanes(right, inside), along_lanes(left, inside))
            result = jnp.where(group == q, picked, result)
        pair_out[:, part, :] = result


G_SHAPE = jax.ShapeDtypeStruct((2, B, B), F32)


def first(e, eta, head):
    return pl.pallas_call(
        first_body,
        out_shape=G_SHAPE,
        in_specs=[SMEM, SMEM, VMEM],
        out_specs=VMEM,
        scratch_shapes=[pltpu.VMEM((B, B), F32)],
        compiler_params=PARAMS,
        name="first",
    )(e, eta, head)


def middle(distance, e, eta, mine, other, g):
    return pl.pallas_call(
        functools.partial(middle_body, distance),
        out_shape=G_SHAPE,
        in_specs=[SMEM, SMEM, VMEM, VMEM, VMEM],
        out_specs=VMEM,
        scratch_shapes=[pltpu.VMEM((PAYLOAD, B), F32), pltpu.VMEM((B, B), F32)],
        compiler_params=PARAMS,
        name="middle",
    )(e, eta, mine, other, g)


def last(e, eta, hamiltonian, coupling, g, near):
    return pl.pallas_call(
        last_body,
        out_shape=(G_SHAPE, G_SHAPE, jax.ShapeDtypeStruct((ROWS, 2, 128), F32)),
        in_specs=[SMEM, SMEM, VMEM, VMEM, VMEM, VMEM],
        out_specs=(VMEM, VMEM, VMEM),
        scratch_shapes=[pltpu.VMEM((2, B, HALF), F32)],
        compiler_params=PARAMS,
        name="last",
    )(e, eta, hamiltonian, coupling, g, near)


def tables_body(near_ref, mode_ref, d_ref, near_out, mode_out, inverse_out, next_out, rounds_out, weight_out, wide):
    wide[0, :, :NEIGH] = near_ref[...].T
    wide[1, :, :NEIGH] = mode_ref[...].T
    near_parts, mode_parts = (
        [wide[w, pl.ds(q, ROWS, stride=GROUPS), :][:, :NEIGH] for q in range(GROUPS)] for w in range(2)
    )
    near = jnp.concatenate(near_parts, axis=1)
    near_out[...] = near
    modes = jnp.concatenate(mode_parts, axis=1)
    y, z, core = (lax.axis_index(a) for a in ENERGY)
    mine = (y * lax.axis_size("z") + z) * lax.axis_size("core") + core
    own = jnp.where(iota((ROWS, 128), 0) == mine, modes, 0)
    mode_out[...] = jnp.broadcast_to(jnp.sum(own, axis=0, keepdims=True), (8, 128))
    column = iota((ROWS, B), 1)
    for q in range(GROUPS):
        table = jnp.full((ROWS, B), -1, jnp.int32)
        for k in reversed(range(NEIGH)):
            table = jnp.where(near_parts[q][:, k : k + 1] == column, q * NEIGH + k, table)
        inverse_out[q * ROWS : (q + 1) * ROWS, :] = table
    lane = iota((ROWS, 128), 1)
    place = jnp.bitwise_and(lane, NEIGH - 1)
    follower = jnp.full((ROWS, 128), -1, jnp.int32)
    count = jnp.zeros((ROWS, 128), F32)
    for shift in reversed(range(1, NEIGH)):
        same = (pltpu.roll(near, 128 - shift, axis=1) == near) & (place + shift < NEIGH)
        follower = jnp.where(same, lane + shift, follower)
        count = count + jnp.where(same, 1.0, 0.0)
    next_out[...] = follower
    rounds_out[...] = jnp.broadcast_to(jnp.max(count, axis=0, keepdims=True), (8, 128))
    scale = 2.0 * math.sqrt(B / NEIGH)
    modes_count, energies = d_ref.shape[1], d_ref.shape[2]
    size = 2 * energies
    total = modes_count * size
    for m in range(modes_count):
        real = scale * d_ref[0, m]
        imag = scale * d_ref[1, m]
        top = jnp.concatenate([real, -imag], axis=1)
        bottom = jnp.concatenate([imag, real], axis=1)
        high, low = split(jnp.concatenate([top, bottom], axis=0))
        weight_out[:, m * size : (m + 1) * size] = high
        weight_out[:, total + m * size : total + (m + 1) * size] = high
        weight_out[:, 2 * total + m * size : 2 * total + (m + 1) * size] = low


def tables(neighbors, phonon_modes, propagator):
    modes_count, energies = propagator.shape[1:3]
    return pl.pallas_call(
        tables_body,
        out_shape=(
            jax.ShapeDtypeStruct((ROWS, 128), jnp.int32),
            jax.ShapeDtypeStruct((8, 128), jnp.int32),
            jax.ShapeDtypeStruct((B, B), jnp.int32),
            jax.ShapeDtypeStruct((ROWS, 128), jnp.int32),
            jax.ShapeDtypeStruct((8, 128), F32),
            jax.ShapeDtypeStruct((2 * energies, 6 * modes_count * energies), BF16),
        ),
        in_specs=[VMEM, VMEM, VMEM],
        out_specs=(VMEM, VMEM, VMEM, VMEM, VMEM, VMEM),
        scratch_shapes=[pltpu.VMEM((2, B, 128), jnp.int32)],
        compiler_params=PARAMS,
        name="tables",
    )(neighbors, phonon_modes, propagator)


def convolve_body(modes_count, weight_ref, mode_ref, green_ref, out_ref):
    stacked = jnp.concatenate([green_ref[:, 0, :], green_ref[:, 1, :]], axis=0)
    high, low = (x.astype(F32) for x in split(stacked))
    mode = mode_ref[0:1, :]
    highs, lows = [], []
    for m in range(modes_count):
        highs.append(jnp.where(mode == m, high, 0.0).astype(BF16))
        lows.append(jnp.where(mode == m, low, 0.0).astype(BF16))
    right = jnp.concatenate(highs + lows + highs, axis=0)
    result = jnp.dot(weight_ref[...], right, preferred_element_type=F32)
    energies = green_ref.shape[0]
    out_ref[:, 0, :] = result[:energies]
    out_ref[:, 1, :] = result[energies:]


def convolve(modes_count, weight, mode, green):
    return pl.pallas_call(
        functools.partial(convolve_body, modes_count),
        out_shape=jax.ShapeDtypeStruct(green.shape, F32),
        in_specs=[VMEM, VMEM, VMEM],
        out_specs=VMEM,
        compiler_params=PARAMS,
        name="convolve",
    )(weight, mode, green)


def correct_body(
    rounds_ref, self_ref, next_ref, inverse_ref, g_ref, p_ref, out_ref, self_out, moved, result, sems
):
    pass_on = pltpu.make_async_copy(self_ref, self_out, sems.at[0])
    pass_on.start()
    part_real = self_ref[:, 0, :]
    part_imag = self_ref[:, 1, :]
    follower = next_ref[...]

    def gather_round(_, carry):
        sum_real, sum_imag, pointer = carry
        valid = pointer >= 0
        index = jnp.maximum(pointer, 0)
        sum_real = sum_real + jnp.where(valid, along_lanes(part_real, index), 0.0)
        sum_imag = sum_imag + jnp.where(valid, along_lanes(part_imag, index), 0.0)
        return sum_real, sum_imag, jnp.where(valid, along_lanes(follower, index), -1)

    sum_real, sum_imag, _ = lax.fori_loop(
        0, jnp.max(rounds_ref[...]).astype(jnp.int32), gather_round, (part_real, part_imag, follower)
    )
    reals, imags = [], []
    for q in range(GROUPS):
        row_real, row_imag = [], []
        for side in range(2):
            table = inverse_ref[q * ROWS : (q + 1) * ROWS, side * HALF : (side + 1) * HALF]
            valid = table >= 0
            index = jnp.maximum(table, 0)
            row_real.append(jnp.where(valid, along_lanes(sum_real, index), 0.0))
            row_imag.append(jnp.where(valid, along_lanes(sum_imag, index), 0.0))
        reals.append(jnp.concatenate(row_real, axis=1))
        imags.append(jnp.concatenate(row_imag, axis=1))
    sigma_real = jnp.concatenate(reals, axis=0)
    sigma_imag = jnp.concatenate(imags, axis=0)
    g_real, g_imag = g_ref[0], g_ref[1]
    s_real, s_imag = complex_product(thirds(sigma_real, sigma_imag), thirds(g_real, g_imag))
    for q in range(GROUPS):
        rows = slice(q * ROWS, (q + 1) * ROWS)
        for part, value in enumerate((s_real, s_imag)):
            for side in range(2):
                piece = value[rows, side * HALF : (side + 1) * HALF]
                moved[2 * part + side, pl.ds(q, ROWS, stride=GROUPS), :] = piece
    moved_real = jnp.concatenate([moved[0], moved[1]], axis=1)
    moved_imag = jnp.concatenate([moved[2], moved[3]], axis=1)
    p_thirds = thirds(p_ref[0], p_ref[1])
    square_real, square_imag = complex_product(p_thirds, p_thirds)
    right = thirds(square_real + moved_real, square_imag + moved_imag)
    leaving = []
    for half in range(2):
        rows = slice(half * HALF, (half + 1) * HALF)
        add_real, add_imag = complex_product(thirds(g_real[rows], g_imag[rows]), right)
        result[0, rows, :] = g_real[rows] + add_real
        result[1, rows, :] = g_imag[rows] + add_imag
        out = pltpu.make_async_copy(result.at[:, rows, :], out_ref.at[0, :, rows, :], sems.at[1 + half])
        out.start()
        leaving.append(out)
    pass_on.wait()
    for out in leaving:
        out.wait()


def correct(rounds, self_part, follower, inverse, g, p):
    return pl.pallas_call(
        correct_body,
        out_shape=(
            jax.ShapeDtypeStruct((1, 2, B, B), F32),
            jax.ShapeDtypeStruct(self_part.shape, F32),
        ),
        in_specs=[VMEM] * 6,
        out_specs=(HBM, HBM),
        scratch_shapes=[
            pltpu.VMEM((4, B, HALF), F32),
            pltpu.VMEM((2, B, B), F32),
            pltpu.SemaphoreType.DMA((3,)),
        ],
        compiler_params=PARAMS,
        name="correct",
    )(rounds, self_part, follower, inverse, g, p)


def shifted(x, distance):
    count = lax.axis_size("slab")
    return lax.ppermute(x, "slab", [(i, (i + distance) % count) for i in range(count)])


def body(energies, broadening, hamiltonian, coupling, propagator, neighbors, phonon_modes):
    swap = [(0, 1), (1, 0)]
    head, piece = pack(hamiltonian, coupling)
    far = shifted(piece, 2)
    head0 = shifted(head, 3)
    close = shifted(piece, 1)
    far_other = lax.ppermute(far, "core", swap)
    close_other = lax.ppermute(close, "core", swap)
    near, mode, inverse, follower, rounds, weight = tables(neighbors.T, phonon_modes.T, propagator)
    g = first(energies, broadening, head0)
    g = middle(2, energies, broadening, far, far_other, g)
    g = middle(1, energies, broadening, close, close_other, g)
    g, p, pairs = last(energies, broadening, hamiltonian, coupling, g, near)
    regrouped = lax.all_to_all(pairs, ENERGY, 0, 0, tiled=True)
    owned = convolve(propagator.shape[1], weight, mode, regrouped)
    returned = lax.all_to_all(owned, ENERGY, 0, 0, tiled=True)
    green, self_part = correct(rounds, returned, follower, inverse, g, p)
    self_part = jnp.swapaxes(self_part, 0, 1).reshape(1, 2, B * NEIGH)
    return green, self_part


def solution(mesh):
    finer = Mesh(mesh.devices.reshape(mesh.shape["slab"], 4, 8, 2), ("slab", *ENERGY))
    in_specs = (
        P(ENERGY),
        P(ENERGY),
        P("slab", None),
        P("slab", None),
        P(),
        P("slab", None),
        P("slab", None),
    )
    out_specs = (P(ENERGY, None, "slab", None), P(ENERGY, None, "slab"))
    return jax.shard_map(body, mesh=finer, in_specs=in_specs, out_specs=out_specs, check_vma=False)
```

```python
import functools
import math

import jax
import jax.numpy as jnp
from jax import lax
from jax.experimental import pallas as pl
from jax.experimental.pallas import tpu as pltpu
from jax.sharding import Mesh
from jax.sharding import PartitionSpec as P


B = 256
HALF = B // 2
NEIGH = 32
ENERGY = ("y", "z", "core")
PACKED_H = HALF + 16
PAYLOAD = PACKED_H + B
PIECE = PAYLOAD // 2
HEAD = PACKED_H // 2
GROUPS = 4
CHAIN = 3
ROWS = B // GROUPS
F32 = jnp.float32
BF16 = jnp.bfloat16
VMEM = pl.BlockSpec(memory_space=pltpu.VMEM)
SMEM = pl.BlockSpec(memory_space=pltpu.SMEM)
HBM = pl.BlockSpec(memory_space=pltpu.HBM)
PARAMS = pltpu.CompilerParams(vmem_limit_bytes=16 * 1024 * 1024)


def iota(shape, dim):
    return lax.broadcasted_iota(jnp.int32, shape, dim)


def split(x):
    high = x.astype(BF16)
    return high, (x - high.astype(F32)).astype(BF16)


def dot(left, right):
    return jnp.dot(left, right, preferred_element_type=F32)


def dot_turned(left, right):
    return lax.dot_general(left, right, (((1,), (1,)), ((), ())), preferred_element_type=F32)


def three_passes(left, right, multiply=dot):
    high, low = left
    return multiply(high, right[0]) + multiply(low, right[0]) + multiply(high, right[1])


def thirds(real, imag):
    return split(real), split(imag), split(real + imag)


def complex_product(left, right):
    first, second, mixed = (three_passes(x, y) for x, y in zip(left, right))
    return first - second, mixed - first - second


def pack_body(h_ref, c_ref, head_out, piece_ref, h, head_ref, sems):
    core = lax.axis_index("core")
    load = pltpu.make_async_copy(h_ref, h, sems.at[0])
    load.start()
    first_rows = PIECE - PACKED_H
    begin = pltpu.make_async_copy(
        c_ref.at[pl.ds(0, first_rows)], piece_ref.at[pl.ds(PACKED_H, first_rows)], sems.at[1]
    )
    rest = pltpu.make_async_copy(c_ref.at[pl.ds(first_rows, PIECE)], piece_ref, sems.at[1])

    @pl.when(core == 0)
    def _():
        begin.start()

    @pl.when(core != 0)
    def _():
        rest.start()

    load.wait()
    row = iota((HALF, HALF), 0)
    col = iota((HALF, HALF), 1)
    lower = h[HALF:, HALF:]
    head_ref[:HALF, :HALF] = jnp.where(row <= col, h[:HALF, :HALF], lower)
    head_ref[:HALF, HALF:] = h[:HALF, HALF:]
    diagonal = jnp.sum(jnp.where(row == col, lower, 0.0), axis=0, keepdims=True)
    head_ref[HALF:PACKED_H, :HALF] = jnp.broadcast_to(diagonal, (PACKED_H - HALF, HALF))
    head_ref[HALF:PACKED_H, HALF:] = jnp.zeros((PACKED_H - HALF, HALF), F32)

    @pl.when(core == 0)
    def _():
        piece_ref[:PACKED_H, :] = head_ref[...]
        head_out[...] = head_ref[:HEAD, :]
        begin.wait()

    @pl.when(core != 0)
    def _():
        head_out[...] = head_ref[HEAD:, :]
        rest.wait()


def pack(hamiltonian, coupling):
    return pl.pallas_call(
        pack_body,
        out_shape=(
            jax.ShapeDtypeStruct((HEAD, B), F32),
            jax.ShapeDtypeStruct((PIECE, B), F32),
        ),
        in_specs=[HBM, HBM],
        out_specs=(VMEM, VMEM),
        scratch_shapes=[
            pltpu.VMEM((B, B), F32),
            pltpu.VMEM((PACKED_H, B), F32),
            pltpu.SemaphoreType.DMA((2,)),
        ],
        compiler_params=PARAMS,
        name="pack",
    )(*(pltpu.with_memory_space_constraint(x, pltpu.HBM) for x in (hamiltonian, coupling)))


def unpack_h(packed_ref, h):
    row = iota((HALF, HALF), 0)
    col = iota((HALF, HALF), 1)
    mixed = packed_ref[:HALF, :HALF]
    turned = mixed.T
    across = packed_ref[:HALF, HALF:]
    h[:HALF, :HALF] = jnp.where(row <= col, mixed, turned)
    h[:HALF, HALF:] = across
    h[HALF:, :HALF] = across.T
    last = jnp.where(row > col, mixed, turned)
    diagonal = packed_ref[HALF : HALF + 1, :HALF]
    h[HALF:, HALF:] = jnp.where(row == col, diagonal, last)


def stage_math(stage, e_ref, eta_ref, h, c, g_in, g_out, p_out):
    row = iota((B, B), 0)
    col = iota((B, B), 1)
    on = row == col

    def finish(negated_real, negated_imag):
        full_real = jnp.where(on, e_ref[0], 0.0) - negated_real
        diag_real = jnp.sum(jnp.where(on, full_real, 0.0), axis=0, keepdims=True)
        side_real = jnp.sum(jnp.where(on, full_real, 0.0), axis=1, keepdims=True)
        if negated_imag is None:
            diag_imag = jnp.full((1, B), eta_ref[0], F32)
            side_imag = jnp.full((B, 1), eta_ref[0], F32)
        else:
            full_imag = jnp.where(on, eta_ref[0], 0.0) - negated_imag
            diag_imag = jnp.sum(jnp.where(on, full_imag, 0.0), axis=0, keepdims=True)
            side_imag = jnp.sum(jnp.where(on, full_imag, 0.0), axis=1, keepdims=True)

        def reciprocal(real, imag):
            modulus = real * real + imag * imag
            return real / modulus, -imag / modulus

        row_real, row_imag = reciprocal(diag_real, diag_imag)
        col_real, col_imag = reciprocal(side_real, side_imag)
        n_real = jnp.where(on, 0.0, -negated_real)
        outer_real = col_real * row_real - col_imag * row_imag
        outer_imag = col_real * row_imag + col_imag * row_real
        if negated_imag is None:
            z_real = outer_real * n_real
            z_imag = outer_imag * n_real
            n_split = split(n_real)
            p_real, p_imag = (three_passes(n_split, split(z)) for z in (z_real, z_imag))
        else:
            n_imag = jnp.where(on, 0.0, -negated_imag)
            z_real = outer_real * n_real - outer_imag * n_imag
            z_imag = outer_real * n_imag + outer_imag * n_real
            p_real, p_imag = complex_product(thirds(n_real, n_imag), thirds(z_real, z_imag))
        x_real = jnp.where(on, row_real, 0.0) - z_real
        x_imag = jnp.where(on, row_imag, 0.0) - z_imag
        add_real, add_imag = complex_product(thirds(x_real, x_imag), thirds(p_real, p_imag))
        g_out[0] = x_real + add_real
        g_out[1] = x_imag + add_imag
        if p_out is not None:
            p_out[0] = p_real
            p_out[1] = p_imag

    @pl.when(stage == 0)
    def _():
        finish(h[...], None)

    if g_in is not None:

        @pl.when(stage > 0)
        def _():
            c_split = split(c[...])
            u_real, u_imag = (
                three_passes(split(three_passes(c_split, split(g_in[part]))), c_split, dot_turned)
                for part in range(2)
            )
            finish(h[...] + u_real, u_imag)


def join(mine_ref, other_ref, whole):
    core = lax.axis_index("core")
    rows = mine_ref.shape[0]
    whole[pl.ds(pl.multiple_of(core * rows, 8), rows), :] = mine_ref[...]
    whole[pl.ds(pl.multiple_of((1 - core) * rows, 8), rows), :] = other_ref[...]


def first_body(e_ref, eta_ref, mine_ref, other_ref, g_out, packed, h):
    stage = lax.axis_index("slab") - 3

    @pl.when(stage >= 0)
    def _():
        join(mine_ref, other_ref, packed)
        unpack_h(packed, h)
        stage_math(stage, e_ref, eta_ref, h, None, None, g_out, None)


def middle_body(distance, e_ref, eta_ref, mine_ref, other_ref, g_in, g_out, payload, h):
    stage = lax.axis_index("slab") - distance

    @pl.when(stage >= 0)
    def _():
        join(mine_ref, other_ref, payload)
        unpack_h(payload, h)
        stage_math(stage, e_ref, eta_ref, h, payload.at[PACKED_H:, :], g_in, g_out, None)


def along_lanes(x, index):
    return jnp.take_along_axis(x, index, axis=1)


def last_body(e_ref, eta_ref, _, h_ref, c_ref, g_in, near_ref, g_out, p_out, pair_out, halves):
    stage_math(lax.axis_index("slab"), e_ref, eta_ref, h_ref, c_ref, g_in, g_out, p_out)
    near = near_ref[...]
    inside = jnp.bitwise_and(near, HALF - 1)
    upper = near >= HALF
    group = iota((ROWS, 128), 1) // NEIGH
    for part in range(2):
        halves[2 * part] = g_out[part, :, :HALF]
        halves[2 * part + 1] = g_out[part, :, HALF:]
        result = jnp.zeros((ROWS, 128), F32)
        for q in range(GROUPS):
            left = halves[2 * part, pl.ds(q, ROWS, stride=GROUPS), :]
            right = halves[2 * part + 1, pl.ds(q, ROWS, stride=GROUPS), :]
            picked = jnp.where(upper, along_lanes(right, inside), along_lanes(left, inside))
            result = jnp.where(group == q, picked, result)
        pair_out[:, part, :] = result


G_SHAPE = jax.ShapeDtypeStruct((2, B, B), F32)


def first(e, eta, mine, other):
    return pl.pallas_call(
        first_body,
        out_shape=G_SHAPE,
        in_specs=[SMEM, SMEM, VMEM, VMEM],
        out_specs=VMEM,
        scratch_shapes=[pltpu.VMEM((PACKED_H, B), F32), pltpu.VMEM((B, B), F32)],
        compiler_params=PARAMS,
        name="first",
    )(e, eta, mine, other)


def middle(distance, e, eta, mine, other, g):
    return pl.pallas_call(
        functools.partial(middle_body, distance),
        out_shape=G_SHAPE,
        in_specs=[SMEM, SMEM, VMEM, VMEM, VMEM],
        out_specs=VMEM,
        scratch_shapes=[pltpu.VMEM((PAYLOAD, B), F32), pltpu.VMEM((B, B), F32)],
        compiler_params=PARAMS,
        name="middle",
    )(e, eta, mine, other, g)


def last(e, eta, rounds, hamiltonian, coupling, g, near):
    return pl.pallas_call(
        last_body,
        out_shape=(G_SHAPE, G_SHAPE, jax.ShapeDtypeStruct((ROWS, 2, 128), F32)),
        in_specs=[SMEM, SMEM, SMEM, VMEM, VMEM, VMEM, VMEM],
        out_specs=(VMEM, VMEM, VMEM),
        scratch_shapes=[pltpu.VMEM((4, B, HALF), F32)],
        compiler_params=PARAMS,
        name="last",
    )(e, eta, rounds, hamiltonian, coupling, g, near)


def tables_body(near_ref, mode_ref, d_ref, near_out, mode_out, inverse_out, next_out, rounds_out, weight_out, wide):
    wide[0, :, :NEIGH] = near_ref[...].T
    wide[1, :, :NEIGH] = mode_ref[...].T
    near_parts, mode_parts = (
        [wide[w, pl.ds(q, ROWS, stride=GROUPS), :][:, :NEIGH] for q in range(GROUPS)] for w in range(2)
    )
    near = jnp.concatenate(near_parts, axis=1)
    near_out[...] = near
    modes = jnp.concatenate(mode_parts, axis=1)
    y, z, core = (lax.axis_index(a) for a in ENERGY)
    mine = (y * lax.axis_size("z") + z) * lax.axis_size("core") + core
    own = jnp.where(iota((ROWS, 128), 0) == mine, modes, 0)
    mode_out[...] = jnp.broadcast_to(jnp.sum(own, axis=0, keepdims=True), (8, 128))
    column = iota((ROWS, B), 1)
    for q in range(GROUPS):
        table = jnp.full((ROWS, B), -1, jnp.int32)
        for k in reversed(range(NEIGH)):
            table = jnp.where(near_parts[q][:, k : k + 1] == column, q * NEIGH + k, table)
        inverse_out[q * ROWS : (q + 1) * ROWS, :] = table
    lane = iota((ROWS, 128), 1)
    place = jnp.bitwise_and(lane, NEIGH - 1)
    follower = jnp.full((ROWS, 128), -1, jnp.int32)
    count = jnp.zeros((ROWS, 128), F32)
    for shift in reversed(range(1, NEIGH)):
        same = (pltpu.roll(near, 128 - shift, axis=1) == near) & (place + shift < NEIGH)
        follower = jnp.where(same, lane + shift, follower)
        count = count + jnp.where(same, 1.0, 0.0)
    chain = follower
    for step in range(CHAIN):
        next_out[step] = chain
        beyond = along_lanes(follower, jnp.maximum(chain, 0))
        chain = jnp.where(chain >= 0, beyond, -1)
    rounds_out[...] = jnp.broadcast_to(jnp.max(count, axis=0, keepdims=True), (8, 128))
    scale = 2.0 * math.sqrt(B / NEIGH)
    modes_count, energies = d_ref.shape[1], d_ref.shape[2]
    size = 2 * energies
    total = modes_count * size
    for m in range(modes_count):
        real = scale * d_ref[0, m]
        imag = scale * d_ref[1, m]
        top = jnp.concatenate([real, -imag], axis=1)
        bottom = jnp.concatenate([imag, real], axis=1)
        high, low = split(jnp.concatenate([top, bottom], axis=0))
        weight_out[:, m * size : (m + 1) * size] = high
        weight_out[:, total + m * size : total + (m + 1) * size] = high
        weight_out[:, 2 * total + m * size : 2 * total + (m + 1) * size] = low


def tables(neighbors, phonon_modes, propagator):
    modes_count, energies = propagator.shape[1:3]
    return pl.pallas_call(
        tables_body,
        out_shape=(
            jax.ShapeDtypeStruct((ROWS, 128), jnp.int32),
            jax.ShapeDtypeStruct((8, 128), jnp.int32),
            jax.ShapeDtypeStruct((B, B), jnp.int32),
            jax.ShapeDtypeStruct((CHAIN, ROWS, 128), jnp.int32),
            jax.ShapeDtypeStruct((8, 128), F32),
            jax.ShapeDtypeStruct((2 * energies, 6 * modes_count * energies), BF16),
        ),
        in_specs=[VMEM, VMEM, VMEM],
        out_specs=(VMEM, VMEM, VMEM, VMEM, VMEM, VMEM),
        scratch_shapes=[pltpu.VMEM((2, B, 128), jnp.int32)],
        compiler_params=PARAMS,
        name="tables",
    )(neighbors, phonon_modes, propagator)


def convolve_body(modes_count, weight_ref, mode_ref, green_ref, out_ref):
    stacked = jnp.concatenate([green_ref[:, 0, :], green_ref[:, 1, :]], axis=0)
    high, low = (x.astype(F32) for x in split(stacked))
    mode = mode_ref[0:1, :]
    highs, lows = [], []
    for m in range(modes_count):
        highs.append(jnp.where(mode == m, high, 0.0).astype(BF16))
        lows.append(jnp.where(mode == m, low, 0.0).astype(BF16))
    right = jnp.concatenate(highs + lows + highs, axis=0)
    result = jnp.dot(weight_ref[...], right, preferred_element_type=F32)
    energies = green_ref.shape[0]
    out_ref[:, 0, :] = result[:energies]
    out_ref[:, 1, :] = result[energies:]


def convolve(modes_count, weight, mode, green):
    return pl.pallas_call(
        functools.partial(convolve_body, modes_count),
        out_shape=jax.ShapeDtypeStruct(green.shape, F32),
        in_specs=[VMEM, VMEM, VMEM],
        out_specs=VMEM,
        compiler_params=PARAMS,
        name="convolve",
    )(weight, mode, green)


def correct_body(
    rounds_ref, self_ref, next_ref, inverse_ref, g_ref, p_ref, out_ref, self_out, moved, result, sems
):
    pass_on = pltpu.make_async_copy(self_ref, self_out, sems.at[0])
    pass_on.start()
    part_real = self_ref[:, 0, :]
    part_imag = self_ref[:, 1, :]

    def gather_round(sum_real, sum_imag, pointer):
        valid = pointer >= 0
        index = jnp.maximum(pointer, 0)
        sum_real = sum_real + jnp.where(valid, along_lanes(part_real, index), 0.0)
        sum_imag = sum_imag + jnp.where(valid, along_lanes(part_imag, index), 0.0)
        return sum_real, sum_imag

    def later_round(_, carry):
        sum_real, sum_imag, pointer = carry
        beyond = along_lanes(next_ref[0], jnp.maximum(pointer, 0))
        pointer = jnp.where(pointer >= 0, beyond, -1)
        return *gather_round(sum_real, sum_imag, pointer), pointer

    sum_real, sum_imag = part_real, part_imag
    for step in range(CHAIN):
        sum_real, sum_imag = gather_round(sum_real, sum_imag, next_ref[step])
    sum_real, sum_imag, _ = lax.fori_loop(
        CHAIN, rounds_ref[0], later_round, (sum_real, sum_imag, next_ref[CHAIN - 1])
    )
    reals, imags = [], []
    for q in range(GROUPS):
        row_real, row_imag = [], []
        for side in range(2):
            table = inverse_ref[q * ROWS : (q + 1) * ROWS, side * HALF : (side + 1) * HALF]
            valid = table >= 0
            index = jnp.maximum(table, 0)
            row_real.append(jnp.where(valid, along_lanes(sum_real, index), 0.0))
            row_imag.append(jnp.where(valid, along_lanes(sum_imag, index), 0.0))
        reals.append(jnp.concatenate(row_real, axis=1))
        imags.append(jnp.concatenate(row_imag, axis=1))
    sigma_real = jnp.concatenate(reals, axis=0)
    sigma_imag = jnp.concatenate(imags, axis=0)
    g_real, g_imag = g_ref[0], g_ref[1]
    s_real, s_imag = complex_product(thirds(sigma_real, sigma_imag), thirds(g_real, g_imag))
    for q in range(GROUPS):
        rows = slice(q * ROWS, (q + 1) * ROWS)
        for part, value in enumerate((s_real, s_imag)):
            for side in range(2):
                piece = value[rows, side * HALF : (side + 1) * HALF]
                moved[2 * part + side, pl.ds(q, ROWS, stride=GROUPS), :] = piece
    moved_real = jnp.concatenate([moved[0], moved[1]], axis=1)
    moved_imag = jnp.concatenate([moved[2], moved[3]], axis=1)
    p_thirds = thirds(p_ref[0], p_ref[1])
    square_real, square_imag = complex_product(p_thirds, p_thirds)
    right = thirds(square_real + moved_real, square_imag + moved_imag)
    left = thirds(g_real, g_imag)
    first = three_passes(left[0], right[0])
    second = three_passes(left[1], right[1])
    result[0] = g_real + (first - second)
    leave_real = pltpu.make_async_copy(result.at[0], out_ref.at[0, 0], sems.at[1])
    leave_real.start()
    result[1] = g_imag + (three_passes(left[2], right[2]) - first - second)
    leave_imag = pltpu.make_async_copy(result.at[1], out_ref.at[0, 1], sems.at[2])
    leave_imag.start()
    pass_on.wait()
    leave_real.wait()
    leave_imag.wait()


def correct(rounds, self_part, follower, inverse, g, p):
    return pl.pallas_call(
        correct_body,
        out_shape=(
            jax.ShapeDtypeStruct((1, 2, B, B), F32),
            jax.ShapeDtypeStruct(self_part.shape, F32),
        ),
        in_specs=[SMEM] + [VMEM] * 5,
        out_specs=(HBM, HBM),
        scratch_shapes=[
            pltpu.VMEM((4, B, HALF), F32),
            pltpu.VMEM((2, B, B), F32),
            pltpu.SemaphoreType.DMA((3,)),
        ],
        compiler_params=PARAMS,
        name="correct",
    )(rounds, self_part, follower, inverse, g, p)


def shifted(x, distance):
    count = lax.axis_size("slab")
    return lax.ppermute(x, "slab", [(i, (i + distance) % count) for i in range(count)])


def body(energies, broadening, hamiltonian, coupling, propagator, neighbors, phonon_modes):
    swap = [(0, 1), (1, 0)]
    head, piece = pack(hamiltonian, coupling)
    far = lax.ppermute(piece, "slab", [(0, 2), (1, 3), (2, 1), (3, 0)])
    head0 = shifted(head, 3)
    close = shifted(piece, 1)
    far_other = lax.ppermute(far, "core", swap)
    head_other = lax.ppermute(head0, "core", swap)
    close_other = lax.ppermute(close, "core", swap)
    near, mode, inverse, follower, rounds, weight = tables(neighbors.T, phonon_modes.T, propagator)
    rounds = jnp.max(rounds[:1]).astype(jnp.int32).reshape(1)
    g = first(energies, broadening, head0, head_other)
    g = middle(2, energies, broadening, far, far_other, g)
    g = middle(1, energies, broadening, close, close_other, g)
    g, p, pairs = last(energies, broadening, rounds, hamiltonian, coupling, g, near)
    regrouped = lax.all_to_all(pairs, ENERGY, 0, 0, tiled=True)
    owned = convolve(propagator.shape[1], weight, mode, regrouped)
    returned = lax.all_to_all(owned, ENERGY, 0, 0, tiled=True)
    green, self_part = correct(rounds, returned, follower, inverse, g, p)
    self_part = jnp.swapaxes(self_part, 0, 1).reshape(1, 2, B * NEIGH)
    return green, self_part


def solution(mesh):
    finer = Mesh(mesh.devices.reshape(mesh.shape["slab"], 4, 8, 2), ("slab", *ENERGY))
    in_specs = (
        P(ENERGY),
        P(ENERGY),
        P("slab", None),
        P("slab", None),
        P(),
        P("slab", None),
        P("slab", None),
    )
    out_specs = (P(ENERGY, None, "slab", None), P(ENERGY, None, "slab"))
    return jax.shard_map(body, mesh=finer, in_specs=in_specs, out_specs=out_specs, check_vma=False)
```

```python
import functools
import math

import jax
import jax.numpy as jnp
from jax import lax
from jax.experimental import pallas as pl
from jax.experimental.pallas import tpu as pltpu
from jax.sharding import Mesh
from jax.sharding import PartitionSpec as P


B = 256
HALF = B // 2
NEIGH = 32
ENERGY = ("y", "z", "core")
PACKED_H = HALF + 16
PAYLOAD = PACKED_H + B
PIECE = PAYLOAD // 2
HEAD = PACKED_H // 2
GROUPS = 4
CHAIN = 3
ROWS = B // GROUPS
F32 = jnp.float32
BF16 = jnp.bfloat16
VMEM = pl.BlockSpec(memory_space=pltpu.VMEM)
SMEM = pl.BlockSpec(memory_space=pltpu.SMEM)
HBM = pl.BlockSpec(memory_space=pltpu.HBM)
PARAMS = pltpu.CompilerParams(vmem_limit_bytes=16 * 1024 * 1024)


def iota(shape, dim):
    return lax.broadcasted_iota(jnp.int32, shape, dim)


def split(x):
    high = x.astype(BF16)
    return high, (x - high.astype(F32)).astype(BF16)


def dot(left, right):
    return jnp.dot(left, right, preferred_element_type=F32)


def dot_turned(left, right):
    return lax.dot_general(left, right, (((1,), (1,)), ((), ())), preferred_element_type=F32)


def three_passes(left, right, multiply=dot):
    high, low = left
    return multiply(high, right[0]) + multiply(low, right[0]) + multiply(high, right[1])


def thirds(real, imag):
    return split(real), split(imag), split(real + imag)


def complex_product(left, right):
    first, second, mixed = (three_passes(x, y) for x, y in zip(left, right))
    return first - second, mixed - first - second


def pack_body(h_ref, c_ref, head_out, piece_ref, h, head_ref, sems):
    core = lax.axis_index("core")
    load = pltpu.make_async_copy(h_ref, h, sems.at[0])
    load.start()
    first_rows = PIECE - PACKED_H
    begin = pltpu.make_async_copy(
        c_ref.at[pl.ds(0, first_rows)], piece_ref.at[pl.ds(PACKED_H, first_rows)], sems.at[1]
    )
    rest = pltpu.make_async_copy(c_ref.at[pl.ds(first_rows, PIECE)], piece_ref, sems.at[1])

    @pl.when(core == 0)
    def _():
        begin.start()

    @pl.when(core != 0)
    def _():
        rest.start()

    load.wait()
    row = iota((HALF, HALF), 0)
    col = iota((HALF, HALF), 1)
    lower = h[HALF:, HALF:]
    head_ref[:HALF, :HALF] = jnp.where(row <= col, h[:HALF, :HALF], lower)
    head_ref[:HALF, HALF:] = h[:HALF, HALF:]
    diagonal = jnp.sum(jnp.where(row == col, lower, 0.0), axis=0, keepdims=True)
    head_ref[HALF:PACKED_H, :HALF] = jnp.broadcast_to(diagonal, (PACKED_H - HALF, HALF))
    head_ref[HALF:PACKED_H, HALF:] = jnp.zeros((PACKED_H - HALF, HALF), F32)

    @pl.when(core == 0)
    def _():
        piece_ref[:PACKED_H, :] = head_ref[...]
        head_out[...] = head_ref[:HEAD, :]
        begin.wait()

    @pl.when(core != 0)
    def _():
        head_out[...] = head_ref[HEAD:, :]
        rest.wait()


def pack(hamiltonian, coupling):
    return pl.pallas_call(
        pack_body,
        out_shape=(
            jax.ShapeDtypeStruct((HEAD, B), F32),
            jax.ShapeDtypeStruct((PIECE, B), F32),
        ),
        in_specs=[HBM, HBM],
        out_specs=(VMEM, VMEM),
        scratch_shapes=[
            pltpu.VMEM((B, B), F32),
            pltpu.VMEM((PACKED_H, B), F32),
            pltpu.SemaphoreType.DMA((2,)),
        ],
        compiler_params=PARAMS,
        name="pack",
    )(*(pltpu.with_memory_space_constraint(x, pltpu.HBM) for x in (hamiltonian, coupling)))


def unpack_h(packed_ref, h):
    row = iota((HALF, HALF), 0)
    col = iota((HALF, HALF), 1)
    mixed = packed_ref[:HALF, :HALF]
    turned = mixed.T
    across = packed_ref[:HALF, HALF:]
    h[:HALF, :HALF] = jnp.where(row <= col, mixed, turned)
    h[:HALF, HALF:] = across
    h[HALF:, :HALF] = across.T
    last = jnp.where(row > col, mixed, turned)
    diagonal = packed_ref[HALF : HALF + 1, :HALF]
    h[HALF:, HALF:] = jnp.where(row == col, diagonal, last)


def stage_math(stage, e_ref, eta_ref, h, c, g_in, g_out, p_out):
    row = iota((B, B), 0)
    col = iota((B, B), 1)
    on = row == col

    def finish(negated_real, negated_imag):
        full_real = jnp.where(on, e_ref[0], 0.0) - negated_real
        diag_real = jnp.sum(jnp.where(on, full_real, 0.0), axis=0, keepdims=True)
        side_real = jnp.sum(jnp.where(on, full_real, 0.0), axis=1, keepdims=True)
        if negated_imag is None:
            diag_imag = jnp.full((1, B), eta_ref[0], F32)
            side_imag = jnp.full((B, 1), eta_ref[0], F32)
        else:
            full_imag = jnp.where(on, eta_ref[0], 0.0) - negated_imag
            diag_imag = jnp.sum(jnp.where(on, full_imag, 0.0), axis=0, keepdims=True)
            side_imag = jnp.sum(jnp.where(on, full_imag, 0.0), axis=1, keepdims=True)

        def reciprocal(real, imag):
            modulus = real * real + imag * imag
            return real / modulus, -imag / modulus

        row_real, row_imag = reciprocal(diag_real, diag_imag)
        col_real, col_imag = reciprocal(side_real, side_imag)
        n_real = jnp.where(on, 0.0, -negated_real)
        outer_real = col_real * row_real - col_imag * row_imag
        outer_imag = col_real * row_imag + col_imag * row_real
        if negated_imag is None:
            z_real = outer_real * n_real
            z_imag = outer_imag * n_real
            n_split = split(n_real)
            p_real, p_imag = (three_passes(n_split, split(z)) for z in (z_real, z_imag))
        else:
            n_imag = jnp.where(on, 0.0, -negated_imag)
            z_real = outer_real * n_real - outer_imag * n_imag
            z_imag = outer_real * n_imag + outer_imag * n_real
            p_real, p_imag = complex_product(thirds(n_real, n_imag), thirds(z_real, z_imag))
        x_real = jnp.where(on, row_real, 0.0) - z_real
        x_imag = jnp.where(on, row_imag, 0.0) - z_imag
        add_real, add_imag = complex_product(thirds(x_real, x_imag), thirds(p_real, p_imag))
        g_out[0] = x_real + add_real
        g_out[1] = x_imag + add_imag
        if p_out is not None:
            p_out[0] = p_real
            p_out[1] = p_imag

    @pl.when(stage == 0)
    def _():
        finish(h[...], None)

    if g_in is not None:

        @pl.when(stage > 0)
        def _():
            c_split = split(c[...])
            u_real, u_imag = (
                three_passes(split(three_passes(c_split, split(g_in[part]))), c_split, dot_turned)
                for part in range(2)
            )
            finish(h[...] + u_real, u_imag)


def join(mine_ref, other_ref, whole):
    core = lax.axis_index("core")
    rows = mine_ref.shape[0]
    whole[pl.ds(pl.multiple_of(core * rows, 8), rows), :] = mine_ref[...]
    whole[pl.ds(pl.multiple_of((1 - core) * rows, 8), rows), :] = other_ref[...]


def first_body(e_ref, eta_ref, mine_ref, other_ref, g_out, packed, h):
    stage = lax.axis_index("slab") - 3

    @pl.when(stage >= 0)
    def _():
        join(mine_ref, other_ref, packed)
        unpack_h(packed, h)
        stage_math(stage, e_ref, eta_ref, h, None, None, g_out, None)


def middle_body(distance, e_ref, eta_ref, mine_ref, other_ref, g_in, g_out, payload, h):
    stage = lax.axis_index("slab") - distance

    @pl.when(stage >= 0)
    def _():
        join(mine_ref, other_ref, payload)
        unpack_h(payload, h)
        stage_math(stage, e_ref, eta_ref, h, payload.at[PACKED_H:, :], g_in, g_out, None)


def along_lanes(x, index):
    return jnp.take_along_axis(x, index, axis=1)


def last_body(e_ref, eta_ref, _, h_ref, c_ref, g_in, near_ref, g_out, p_out, pair_out, halves):
    stage_math(lax.axis_index("slab"), e_ref, eta_ref, h_ref, c_ref, g_in, g_out, p_out)
    near = near_ref[...]
    inside = jnp.bitwise_and(near, HALF - 1)
    upper = near >= HALF
    group = iota((ROWS, 128), 1) // NEIGH
    for part in range(2):
        halves[2 * part] = g_out[part, :, :HALF]
        halves[2 * part + 1] = g_out[part, :, HALF:]
        result = jnp.zeros((ROWS, 128), F32)
        for q in range(GROUPS):
            left = halves[2 * part, pl.ds(q, ROWS, stride=GROUPS), :]
            right = halves[2 * part + 1, pl.ds(q, ROWS, stride=GROUPS), :]
            picked = jnp.where(upper, along_lanes(right, inside), along_lanes(left, inside))
            result = jnp.where(group == q, picked, result)
        pair_out[:, part, :] = result


G_SHAPE = jax.ShapeDtypeStruct((2, B, B), F32)


def first(e, eta, mine, other):
    return pl.pallas_call(
        first_body,
        out_shape=G_SHAPE,
        in_specs=[SMEM, SMEM, VMEM, VMEM],
        out_specs=VMEM,
        scratch_shapes=[pltpu.VMEM((PACKED_H, B), F32), pltpu.VMEM((B, B), F32)],
        compiler_params=PARAMS,
        name="first",
    )(e, eta, mine, other)


def middle(distance, e, eta, mine, other, g):
    return pl.pallas_call(
        functools.partial(middle_body, distance),
        out_shape=G_SHAPE,
        in_specs=[SMEM, SMEM, VMEM, VMEM, VMEM],
        out_specs=VMEM,
        scratch_shapes=[pltpu.VMEM((PAYLOAD, B), F32), pltpu.VMEM((B, B), F32)],
        compiler_params=PARAMS,
        name="middle",
    )(e, eta, mine, other, g)


def last(e, eta, rounds, hamiltonian, coupling, g, near):
    return pl.pallas_call(
        last_body,
        out_shape=(G_SHAPE, G_SHAPE, jax.ShapeDtypeStruct((ROWS, 2, 128), F32)),
        in_specs=[SMEM, SMEM, SMEM, VMEM, VMEM, VMEM, VMEM],
        out_specs=(VMEM, VMEM, VMEM),
        scratch_shapes=[pltpu.VMEM((4, B, HALF), F32)],
        compiler_params=PARAMS,
        name="last",
    )(e, eta, rounds, hamiltonian, coupling, g, near)


def tables_body(_, __, near_ref, mode_ref, d_ref, near_out, mode_out, inverse_out, next_out, rounds_out, weight_out, wide):
    wide[0, :, :NEIGH] = near_ref[...].T
    wide[1, :, :NEIGH] = mode_ref[...].T
    near_parts, mode_parts = (
        [wide[w, pl.ds(q, ROWS, stride=GROUPS), :][:, :NEIGH] for q in range(GROUPS)] for w in range(2)
    )
    near = jnp.concatenate(near_parts, axis=1)
    near_out[...] = near
    modes = jnp.concatenate(mode_parts, axis=1)
    y, z, core = (lax.axis_index(a) for a in ENERGY)
    mine = (y * lax.axis_size("z") + z) * lax.axis_size("core") + core
    own = jnp.where(iota((ROWS, 128), 0) == mine, modes, 0)
    mode_out[...] = jnp.broadcast_to(jnp.sum(own, axis=0, keepdims=True), (8, 128))
    column = iota((ROWS, B), 1)
    for q in range(GROUPS):
        table = jnp.full((ROWS, B), -1, jnp.int32)
        for k in reversed(range(NEIGH)):
            table = jnp.where(near_parts[q][:, k : k + 1] == column, q * NEIGH + k, table)
        inverse_out[q * ROWS : (q + 1) * ROWS, :] = table
    lane = iota((ROWS, 128), 1)
    place = jnp.bitwise_and(lane, NEIGH - 1)
    follower = jnp.full((ROWS, 128), -1, jnp.int32)
    count = jnp.zeros((ROWS, 128), F32)
    for shift in reversed(range(1, NEIGH)):
        same = (pltpu.roll(near, 128 - shift, axis=1) == near) & (place + shift < NEIGH)
        follower = jnp.where(same, lane + shift, follower)
        count = count + jnp.where(same, 1.0, 0.0)
    chain = follower
    for step in range(CHAIN):
        next_out[step] = chain
        beyond = along_lanes(follower, jnp.maximum(chain, 0))
        chain = jnp.where(chain >= 0, beyond, -1)
    rounds_out[...] = jnp.broadcast_to(jnp.max(count, axis=0, keepdims=True), (8, 128))
    scale = 2.0 * math.sqrt(B / NEIGH)
    modes_count, energies = d_ref.shape[1], d_ref.shape[2]
    size = 2 * energies
    total = modes_count * size
    for m in range(modes_count):
        real = scale * d_ref[0, m]
        imag = scale * d_ref[1, m]
        top = jnp.concatenate([real, -imag], axis=1)
        bottom = jnp.concatenate([imag, real], axis=1)
        high, low = split(jnp.concatenate([top, bottom], axis=0))
        weight_out[:, m * size : (m + 1) * size] = high
        weight_out[:, total + m * size : total + (m + 1) * size] = high
        weight_out[:, 2 * total + m * size : 2 * total + (m + 1) * size] = low


def tables(e, eta, neighbors, phonon_modes, propagator):
    modes_count, energies = propagator.shape[1:3]
    return pl.pallas_call(
        tables_body,
        out_shape=(
            jax.ShapeDtypeStruct((ROWS, 128), jnp.int32),
            jax.ShapeDtypeStruct((8, 128), jnp.int32),
            jax.ShapeDtypeStruct((B, B), jnp.int32),
            jax.ShapeDtypeStruct((CHAIN, ROWS, 128), jnp.int32),
            jax.ShapeDtypeStruct((8, 128), F32),
            jax.ShapeDtypeStruct((2 * energies, 6 * modes_count * energies), BF16),
        ),
        in_specs=[SMEM, SMEM, VMEM, VMEM, VMEM],
        out_specs=(VMEM, VMEM, VMEM, VMEM, VMEM, VMEM),
        scratch_shapes=[pltpu.VMEM((2, B, 128), jnp.int32)],
        compiler_params=PARAMS,
        name="tables",
    )(e, eta, neighbors, phonon_modes, propagator)


def convolve_body(modes_count, weight_ref, mode_ref, green_ref, out_ref):
    stacked = jnp.concatenate([green_ref[:, 0, :], green_ref[:, 1, :]], axis=0)
    high, low = (x.astype(F32) for x in split(stacked))
    mode = mode_ref[0:1, :]
    highs, lows = [], []
    for m in range(modes_count):
        highs.append(jnp.where(mode == m, high, 0.0).astype(BF16))
        lows.append(jnp.where(mode == m, low, 0.0).astype(BF16))
    right = jnp.concatenate(highs + lows + highs, axis=0)
    result = jnp.dot(weight_ref[...], right, preferred_element_type=F32)
    energies = green_ref.shape[0]
    out_ref[:, 0, :] = result[:energies]
    out_ref[:, 1, :] = result[energies:]


def convolve(modes_count, weight, mode, green):
    return pl.pallas_call(
        functools.partial(convolve_body, modes_count),
        out_shape=jax.ShapeDtypeStruct(green.shape, F32),
        in_specs=[VMEM, VMEM, VMEM],
        out_specs=VMEM,
        compiler_params=PARAMS,
        name="convolve",
    )(weight, mode, green)


def correct_body(
    rounds_ref, self_ref, next_ref, inverse_ref, g_ref, p_ref, out_ref, self_out, moved, result, sems
):
    pass_on = pltpu.make_async_copy(self_ref, self_out, sems.at[0])
    pass_on.start()
    p_thirds = thirds(p_ref[0], p_ref[1])
    square_real, square_imag = complex_product(p_thirds, p_thirds)
    part_real = self_ref[:, 0, :]
    part_imag = self_ref[:, 1, :]

    def gather_round(sum_real, sum_imag, pointer):
        valid = pointer >= 0
        index = jnp.maximum(pointer, 0)
        sum_real = sum_real + jnp.where(valid, along_lanes(part_real, index), 0.0)
        sum_imag = sum_imag + jnp.where(valid, along_lanes(part_imag, index), 0.0)
        return sum_real, sum_imag

    def later_round(_, carry):
        sum_real, sum_imag, pointer = carry
        beyond = along_lanes(next_ref[0], jnp.maximum(pointer, 0))
        pointer = jnp.where(pointer >= 0, beyond, -1)
        return *gather_round(sum_real, sum_imag, pointer), pointer

    sum_real, sum_imag = part_real, part_imag
    for step in range(CHAIN):
        sum_real, sum_imag = gather_round(sum_real, sum_imag, next_ref[step])
    sum_real, sum_imag, _ = lax.fori_loop(
        CHAIN, rounds_ref[0], later_round, (sum_real, sum_imag, next_ref[CHAIN - 1])
    )
    reals, imags = [], []
    for q in range(GROUPS):
        row_real, row_imag = [], []
        for side in range(2):
            table = inverse_ref[q * ROWS : (q + 1) * ROWS, side * HALF : (side + 1) * HALF]
            valid = table >= 0
            index = jnp.maximum(table, 0)
            row_real.append(jnp.where(valid, along_lanes(sum_real, index), 0.0))
            row_imag.append(jnp.where(valid, along_lanes(sum_imag, index), 0.0))
        reals.append(jnp.concatenate(row_real, axis=1))
        imags.append(jnp.concatenate(row_imag, axis=1))
    sigma_real = jnp.concatenate(reals, axis=0)
    sigma_imag = jnp.concatenate(imags, axis=0)
    g_real, g_imag = g_ref[0], g_ref[1]
    s_real, s_imag = complex_product(thirds(sigma_real, sigma_imag), thirds(g_real, g_imag))
    for q in range(GROUPS):
        rows = slice(q * ROWS, (q + 1) * ROWS)
        for part, value in enumerate((s_real, s_imag)):
            for side in range(2):
                piece = value[rows, side * HALF : (side + 1) * HALF]
                moved[2 * part + side, pl.ds(q, ROWS, stride=GROUPS), :] = piece
    moved_real = jnp.concatenate([moved[0], moved[1]], axis=1)
    moved_imag = jnp.concatenate([moved[2], moved[3]], axis=1)
    right = thirds(square_real + moved_real, square_imag + moved_imag)
    left = thirds(g_real, g_imag)
    first = three_passes(left[0], right[0])
    second = three_passes(left[1], right[1])
    result[0] = g_real + (first - second)
    leave_real = pltpu.make_async_copy(result.at[0], out_ref.at[0, 0], sems.at[1])
    leave_real.start()
    result[1] = g_imag + (three_passes(left[2], right[2]) - first - second)
    leave_imag = pltpu.make_async_copy(result.at[1], out_ref.at[0, 1], sems.at[2])
    leave_imag.start()
    pass_on.wait()
    leave_real.wait()
    leave_imag.wait()


def correct(rounds, self_part, follower, inverse, g, p):
    return pl.pallas_call(
        correct_body,
        out_shape=(
            jax.ShapeDtypeStruct((1, 2, B, B), F32),
            jax.ShapeDtypeStruct(self_part.shape, F32),
        ),
        in_specs=[SMEM] + [VMEM] * 5,
        out_specs=(HBM, HBM),
        scratch_shapes=[
            pltpu.VMEM((4, B, HALF), F32),
            pltpu.VMEM((2, B, B), F32),
            pltpu.SemaphoreType.DMA((3,)),
        ],
        compiler_params=PARAMS,
        name="correct",
    )(rounds, self_part, follower, inverse, g, p)


def shifted(x, distance):
    count = lax.axis_size("slab")
    return lax.ppermute(x, "slab", [(i, (i + distance) % count) for i in range(count)])


def body(energies, broadening, hamiltonian, coupling, propagator, neighbors, phonon_modes):
    swap = [(0, 1), (1, 0)]
    head, piece = pack(hamiltonian, coupling)
    far = lax.ppermute(piece, "slab", [(0, 2), (1, 3), (2, 1), (3, 0)])
    head0 = shifted(head, 3)
    close = shifted(piece, 1)
    far_other = lax.ppermute(far, "core", swap)
    head_other = lax.ppermute(head0, "core", swap)
    close_other = lax.ppermute(close, "core", swap)
    near, mode, inverse, follower, rounds, weight = tables(
        energies, broadening, neighbors.T, phonon_modes.T, propagator
    )
    rounds = jnp.max(rounds[:1]).astype(jnp.int32).reshape(1)
    g = first(energies, broadening, head0, head_other)
    g = middle(2, energies, broadening, far, far_other, g)
    g = middle(1, energies, broadening, close, close_other, g)
    g, p, pairs = last(energies, broadening, rounds, hamiltonian, coupling, g, near)
    regrouped = lax.all_to_all(pairs, ENERGY, 0, 0, tiled=True)
    owned = convolve(propagator.shape[1], weight, mode, regrouped)
    returned = lax.all_to_all(owned, ENERGY, 0, 0, tiled=True)
    green, self_part = correct(rounds, returned, follower, inverse, g, p)
    self_part = jnp.swapaxes(self_part, 0, 1).reshape(1, 2, B * NEIGH)
    return green, self_part


def solution(mesh):
    finer = Mesh(mesh.devices.reshape(mesh.shape["slab"], 4, 8, 2), ("slab", *ENERGY))
    in_specs = (
        P(ENERGY),
        P(ENERGY),
        P("slab", None),
        P("slab", None),
        P(),
        P("slab", None),
        P("slab", None),
    )
    out_specs = (P(ENERGY, None, "slab", None), P(ENERGY, None, "slab"))
    return jax.shard_map(body, mesh=finer, in_specs=in_specs, out_specs=out_specs, check_vma=False)
```
